32 devices in a mesh: row: 8 (over y, x, core), col: 4 (over z).
Axes of the slice: x: 2, y: 2, z: 4, core: 2. Of those that a mesh axis runs over, the one named last changes fastest.
Arguments:
- resident_inverse: bfloat16 [24576, 24576], P('row', 'col')
- factor: bfloat16 [3, 24576, 512], P(None, 'row', 'col'), may hold values from -0.15625 to 0.15625
- diag_inverse: float32 [3, 512, 512], P(None, None, 'col'), may hold values from -4 to 4
- anc_tiles: int32 [3, 64], replicated, may hold values from -1 to 95, as said below
- slot_tile: int32 [96], replicated, may hold values from 0 to 95, as said below
Outputs:
- new_cols: bfloat16 [3, 24576, 512], P(None, 'row', 'col')
- diag_blocks: float32 [3, 512, 512], P(None, None, 'col')
The draws below stay inside these ranges and needn't reach their ends.
Inputs may be any that keep to these rules, and one draw needn't show every extreme that they name: `anc_tiles`: row j lists the ancestor tiles of supernode j in ascending order, each at most once, followed by -1 in unused entries; every list holds tile 96 - 1; list 0 is full and list 2 has fewer than 32 tiles. A permutation of the tiles; slot s holds tile slot_tile[s], and each tile is stored within the same block of 24 consecutive slots as its own index. `resident_inverse` is symmetric. `resident_inverse` is symmetric.
All inputs are finite; a program needn't handle non-finite values.
Results may differ from the reference program's by a relative error of at most 0.017.
Values may be sent and summed in bfloat16 or wider, within the bound.
A program may use at most 128 MiB of HBM per device.

```python
import jax
import jax.numpy as jnp
from jax import lax

NA = 24576
W = 512
TB = 256
SUPERS = 3
MAXT = 64
NT = 96
OWN_TILES = 24
N_ROW = 8
N_COL = 4


def draw_resident_inverse(key, part):
    key_main = jax.random.fold_in(key, 101)
    spread = 1.5 / NA ** 0.5
    noise = jax.random.normal(key_main, (NA, NA), jnp.float32)
    sym = (noise + noise.T) * (0.70710678 * spread)
    sym = sym + jnp.eye(NA, dtype=jnp.float32)
    return sym.astype(jnp.bfloat16)


def draw_anc_tiles(key, part):
    tile_ids = jnp.arange(NT, dtype=jnp.int32)
    key_pick = jax.random.fold_in(key, 303)
    count_one = jax.random.randint(jax.random.fold_in(key, 404), (), MAXT // 2, MAXT)
    count_two = jax.random.randint(jax.random.fold_in(key, 505), (), MAXT // 4, MAXT // 2)
    counts = jnp.stack([jnp.int32(MAXT), count_one.astype(jnp.int32), count_two.astype(jnp.int32)])
    listing = []
    for which in range(SUPERS):
        raw_scores = jax.random.randint(jax.random.fold_in(key_pick, which), (NT,), 0, NT)
        scores = (raw_scores + tile_ids) * NT + tile_ids
        scores = jnp.where(tile_ids == NT - 1, 4 * NT * NT, scores)
        ranking = jnp.argsort(-scores, stable=True).astype(jnp.int32)
        chosen = ranking[:MAXT]
        in_list = jnp.arange(MAXT, dtype=jnp.int32) < counts[which % 3]
        chosen = jnp.where(in_list, chosen, NT + 1)
        chosen = jnp.sort(chosen)
        listing.append(jnp.where(chosen > NT - 1, -1, chosen).astype(jnp.int32))
    return jnp.stack(listing)


def draw_slot_tile(key, part):
    tile_ids = jnp.arange(NT, dtype=jnp.int32)
    raw_scores = jax.random.randint(jax.random.fold_in(key, 606), (NT,), 0, NT)
    groups = tile_ids // OWN_TILES
    scores = groups * (NT * NT) + raw_scores * NT + tile_ids
    return jnp.argsort(scores, stable=True).astype(jnp.int32)


def strengthened(drawn, rng, source, target, blocks, factor):
    def block_of(position):
        return (jnp.arange(drawn.shape[position]) // (drawn.shape[position] // blocks)).reshape((-1,) + (1,) * (drawn.ndim - 1 - position))

    first = jax.random.permutation(rng, blocks)[block_of(target)]
    far = (block_of(target) + blocks // 2) % blocks
    return jnp.where((block_of(source) == first) | (block_of(source) == far), factor * drawn, drawn)


def steps_of(own_key, extent, pieces, smallest, largest):
    gain = 1.0
    for axis_at, parts in pieces:
        draws = jax.random.uniform(jax.random.fold_in(jax.random.fold_in(own_key, 6), axis_at), (parts,), jnp.float32, smallest / len(pieces), largest / len(pieces))
        gain = gain * jnp.repeat(jnp.exp(draws), extent[axis_at] // parts).reshape((-1,) + (1,) * (len(extent) - 1 - axis_at))
    return gain


def gaussian(key, extent, deviation, limit, shards=(), kind=jnp.bfloat16):
    drawn = deviation * jax.random.normal(key, extent, jnp.float32)
    if shards:
        drawn = drawn * steps_of(key, extent, shards, -0.22, 0.18)
    return jnp.clip(drawn, -limit, limit).astype(kind)


def bell_draw_with(own_key, dims, scale, most, split, heavy, held_as=jnp.bfloat16):
    array = scale * jax.random.normal(own_key, dims, jnp.float32)
    if split:
        array = array * steps_of(own_key, dims, split, -0.22, 0.18)
    return jnp.clip(strengthened(array, jax.random.fold_in(own_key, 3), *heavy), -most, most).astype(held_as)


def setup_inputs(seed: int = 0) -> dict:
    seeds = jax.random.split(jax.random.key(seed), 6)
    resident_inverse = draw_resident_inverse(jax.random.fold_in(seeds[5], 71), 0)
    factor = bell_draw_with(seeds[1], (SUPERS, NA, W), (NA // N_ROW) ** -0.5, 0.15625, ((1, 8), (2, 4)), (1, 2, 8, 2.0))
    diag_inverse = gaussian(seeds[2], (SUPERS, W, W), 0.5, 4.0, ((2, 4),), jnp.float32)
    anc_tiles = draw_anc_tiles(jax.random.fold_in(seeds[5], 71), 0)
    slot_tile = draw_slot_tile(jax.random.fold_in(seeds[5], 71), 0)
    return {"resident_inverse": resident_inverse, "factor": factor, "diag_inverse": diag_inverse, "anc_tiles": anc_tiles, "slot_tile": slot_tile}


def slot_rows(anc_tiles, slot_tile):
    tile_ids = jnp.arange(NT, dtype=jnp.int32)
    listed = jnp.sum((anc_tiles[:, :, None] == tile_ids[None, None, :]).astype(jnp.float32), axis=1)
    onehot = (slot_tile[:, None] == tile_ids[None, :]).astype(jnp.float32)
    slot_mask = jnp.dot(listed, onehot.T, precision=lax.Precision.HIGHEST)
    return jnp.repeat(slot_mask, TB, axis=1)


def reference(resident_inverse, factor, diag_inverse, anc_tiles, slot_tile):
    row_mask = slot_rows(anc_tiles, slot_tile)
    masked = factor * row_mask.astype(jnp.bfloat16)[:, :, None]
    col_width = NA // N_COL

    def add_block(running, column_block):
        offset = column_block * col_width
        columns = lax.dynamic_slice_in_dim(resident_inverse, offset, col_width, 1).astype(jnp.float32)
        picked = lax.dynamic_slice_in_dim(masked, offset, col_width, 1).astype(jnp.float32)
        partial_value = jnp.einsum("rk,skw->srw", columns, picked, precision=lax.Precision.HIGHEST)
        rounded = lax.optimization_barrier(partial_value.astype(jnp.bfloat16))
        return running + rounded.astype(jnp.float32), None

    summed, _ = lax.scan(add_block, jnp.zeros((SUPERS, NA, W), jnp.float32), jnp.arange(N_COL, dtype=jnp.int32))
    new_cols = (-(summed * row_mask[:, :, None])).astype(jnp.bfloat16)
    diag_blocks = diag_inverse + jnp.einsum("snw,snv->swv", masked.astype(jnp.float32), summed, precision=lax.Precision.HIGHEST)
    return new_cols, diag_blocks
```

```python
import jax
import jax.numpy as jnp
from jax import lax
from jax.sharding import PartitionSpec as P


def slot_rows(anc_tiles, slot_tile, tile_rows):
    listed = (anc_tiles[:, :, None] == slot_tile[None, None, :]).any(axis=1)
    return jnp.repeat(listed.astype(jnp.float32), tile_rows, axis=1)


def on_device(resident_inverse, factor, diag_inverse, anc_tiles, slot_tile):
    own_rows, own_cols = resident_inverse.shape
    supers, _, part_width = factor.shape
    row_index = lax.axis_index("row")
    col_index = lax.axis_index("col")
    col_count = lax.axis_size("col")
    row_count = lax.axis_size("row")
    ratio = row_count // col_count
    owners = row_count // ratio
    total_rows = own_rows * row_count
    row_mask = slot_rows(anc_tiles, slot_tile, total_rows // slot_tile.shape[0])
    own_mask = lax.dynamic_slice_in_dim(row_mask, row_index * own_rows, own_rows, 1)
    mine = [factor[s] * own_mask[s].astype(jnp.bfloat16)[:, None] for s in range(supers)]
    last = col_count - 1
    up_moves = [(i, i + 1) for i in range(last)]
    down_moves = [(i + 1, i) for i in range(last)]
    chunk = own_cols // row_count

    parts = []
    for s in range(supers):
        ups, downs = [mine[s]], [mine[s]]
        for by in range(last):
            ups.append(lax.ppermute(ups[-1], "col", up_moves))
            downs.append(lax.ppermute(downs[-1], "col", down_moves))
        parts.append([mine[s]] + [ups[by] + downs[col_count - by] for by in range(1, col_count)])

    news, contribs = [], []
    for s in range(supers):
        wide = jnp.concatenate(parts[s], axis=1)
        partial = lax.dot_general(
            resident_inverse, wide, (((0,), (0,)), ((), ())), preferred_element_type=jnp.float32
        ).astype(jnp.bfloat16)
        summed = lax.psum_scatter(partial, "row", scatter_dimension=0, tiled=True)
        got = [summed[:, :part_width]]
        for by in range(1, col_count):
            piece = summed[:, by * part_width:(by + 1) * part_width]
            got.append(lax.ppermute(piece, "col", [(c, (c - by) % col_count) for c in range(col_count)]))
        got = jnp.stack(got)
        home = []
        for k in range(owners):
            block = (row_index + k) % owners
            piece = lax.dynamic_index_in_dim(got, (block - col_index) % col_count, 0, keepdims=False)
            moves = [(r, ratio * ((r + k) % owners) + r // owners) for r in range(row_count)]
            home.append(lax.ppermute(piece, "row", moves))
        home = jnp.stack(home)
        mine_y = jnp.concatenate([
            lax.dynamic_index_in_dim(home, (row_index // ratio - q) % owners, 0, keepdims=False)
            for q in range(owners)
        ], axis=0)
        news.append(-(mine_y * own_mask[s].astype(jnp.bfloat16)[:, None]))
        contribs.append(jnp.stack([
            jnp.einsum("rw,rv->wv", part, mine_y, preferred_element_type=jnp.float32)
            for part in parts[s]
        ]))
    stacked = jnp.stack(contribs, axis=1)
    ordered = jnp.stack([
        lax.dynamic_index_in_dim(stacked, (col_index - q) % col_count, 0, keepdims=False)
        for q in range(col_count)
    ], axis=1)
    totals = ordered.reshape(supers, col_count * part_width, part_width)
    step = 1
    while step < row_count:
        sent = totals.astype(jnp.bfloat16)
        got = lax.ppermute(sent, "row", [(i, i ^ step) for i in range(row_count)])
        totals = sent.astype(jnp.float32) + got.astype(jnp.float32)
        step *= 2
    return (jnp.stack(news), diag_inverse + totals)


def solution(mesh):
    placed = (P("row", "col"), P(None, "row", "col"), P(None, None, "col"), P(), P())
    return jax.shard_map(
        on_device,
        mesh=mesh,
        in_specs=placed,
        out_specs=(P(None, "row", "col"), P(None, None, "col")),
        check_vma=False,
    )
```

```python
import jax
import jax.numpy as jnp
from jax import lax
from jax.experimental import pallas as pl
from jax.experimental.pallas import tpu as pltpu
from jax.sharding import PartitionSpec as P


def slot_rows(anc_tiles, slot_tile, tile_rows):
    listed = (anc_tiles[:, :, None] == slot_tile[None, None, :]).any(axis=1)
    return jnp.repeat(listed.astype(jnp.float32), tile_rows, axis=1)


def plain(resident_inverse, factor, diag_inverse, anc_tiles, slot_tile):
    own_rows, own_cols = resident_inverse.shape
    supers, _, part_width = factor.shape
    row_index = lax.axis_index("row")
    col_index = lax.axis_index("col")
    col_count = lax.axis_size("col")
    row_count = lax.axis_size("row")
    ratio = row_count // col_count
    owners = row_count // ratio
    total_rows = own_rows * row_count
    row_mask = slot_rows(anc_tiles, slot_tile, total_rows // slot_tile.shape[0])
    own_mask = lax.dynamic_slice_in_dim(row_mask, row_index * own_rows, own_rows, 1)
    mine = [factor[s] * own_mask[s].astype(jnp.bfloat16)[:, None] for s in range(supers)]
    last = col_count - 1
    up_moves = [(i, i + 1) for i in range(last)]
    down_moves = [(i + 1, i) for i in range(last)]
    chunk = own_cols // row_count

    parts = []
    for s in range(supers):
        ups, downs = [mine[s]], [mine[s]]
        for by in range(last):
            ups.append(lax.ppermute(ups[-1], "col", up_moves))
            downs.append(lax.ppermute(downs[-1], "col", down_moves))
        parts.append([mine[s]] + [ups[by] + downs[col_count - by] for by in range(1, col_count)])

    news, contribs = [], []
    for s in range(supers):
        wide = jnp.concatenate(parts[s], axis=1)
        partial = lax.dot_general(
            resident_inverse, wide, (((0,), (0,)), ((), ())), preferred_element_type=jnp.float32
        ).astype(jnp.bfloat16)
        summed = lax.psum_scatter(partial, "row", scatter_dimension=0, tiled=True)
        got = [summed[:, :part_width]]
        for by in range(1, col_count):
            piece = summed[:, by * part_width:(by + 1) * part_width]
            got.append(lax.ppermute(piece, "col", [(c, (c - by) % col_count) for c in range(col_count)]))
        got = jnp.stack(got)
        home = []
        for k in range(owners):
            block = (row_index + k) % owners
            piece = lax.dynamic_index_in_dim(got, (block - col_index) % col_count, 0, keepdims=False)
            moves = [(r, ratio * ((r + k) % owners) + r // owners) for r in range(row_count)]
            home.append(lax.ppermute(piece, "row", moves))
        home = jnp.stack(home)
        mine_y = jnp.concatenate([
            lax.dynamic_index_in_dim(home, (row_index // ratio - q) % owners, 0, keepdims=False)
            for q in range(owners)
        ], axis=0)
        news.append(-(mine_y * own_mask[s].astype(jnp.bfloat16)[:, None]))
        contribs.append(jnp.stack([
            jnp.einsum("rw,rv->wv", part, mine_y, preferred_element_type=jnp.float32)
            for part in parts[s]
        ]))
    stacked = jnp.stack(contribs, axis=1)
    ordered = jnp.stack([
        lax.dynamic_index_in_dim(stacked, (col_index - q) % col_count, 0, keepdims=False)
        for q in range(col_count)
    ], axis=1)
    totals = ordered.reshape(supers, col_count * part_width, part_width)
    step = 1
    while step < row_count:
        sent = totals.astype(jnp.bfloat16)
        got = lax.ppermute(sent, "row", [(i, i ^ step) for i in range(row_count)])
        totals = sent.astype(jnp.float32) + got.astype(jnp.float32)
        step *= 2
    return (jnp.stack(news), diag_inverse + totals)

MESH = pl.DeviceIdType.MESH
BF = jnp.bfloat16
F32 = jnp.float32
CORES = 2
SIDE = 2
CHIPS = SIDE * SIDE


def sweep(row_count, col_count, supers, mine_ref, matrix_ref, y_ref, t_ref,
          slab, parts, to_core, from_core, to_chip, from_chip, block_y, passed, own_y, to_sum, from_sum,
          slab_sem, own_sem, ag_send, ag_recv, core_send, core_recv, chip_send, chip_recv,
          col_send, col_recv, row_send, row_recv, sum_send, sum_recv):
    row = lax.axis_index("row")
    col = lax.axis_index("col")
    last = col_count - 1
    core = row % CORES
    chip = row // CORES
    x, y = chip % SIDE, chip // SIDE
    half = col // 2
    width = parts.shape[2] // 2
    piece = slab.shape[2]
    owners = row_count // CORES
    passes = 2 * supers

    barrier = pltpu.get_barrier_semaphore()

    @pl.loop(1, row_count)
    def _(by):
        pl.semaphore_signal(barrier, inc=1, device_id=((row + by) % row_count, col), device_id_type=MESH)

    @pl.loop(1, col_count)
    def _(by):
        pl.semaphore_signal(barrier, inc=1, device_id=(row, (col + by) % col_count), device_id_type=MESH)

    pl.semaphore_wait(barrier, row_count - 1 + last)

    def to(src, dst, send, recv, r, c):
        return pltpu.make_async_remote_copy(
            src_ref=src, dst_ref=dst, send_sem=send, recv_sem=recv, device_id=(r, c), device_id_type=MESH
        )

    def landed(ref, sem):
        pltpu.make_async_copy(ref, ref, sem).wait()

    def part(s, w):
        return parts.at[s, w // 2, pl.ds(pl.multiple_of((w % 2) * width, width), width), :]

    def gather(s, w, way, src):
        return to(src, part(s, w), ag_send.at[way, s, w], ag_recv.at[s, w], row, col + (1 - 2 * way))

    def chip_at(k):
        xk = (x + 1 - k // 2) % 2
        yk = (y + 1 - k % 2) % 2
        return yk * SIDE + xk

    def slab_copy(k, own, slot):
        which = chip_at(k) * CORES + (core + 1 - own) % CORES
        off = pl.multiple_of(which * piece, piece)
        return pltpu.make_async_copy(matrix_ref.at[:, pl.ds(off, piece)], slab.at[slot], slab_sem.at[slot])

    def own_part(s):
        return pltpu.make_async_copy(mine_ref.at[s], part(s, col), own_sem.at[s])

    slab_copy(0, 0, 0).start()

    @pl.loop(0, supers)
    def _(s):
        @pl.when(col < last)
        def _():
            gather(s, col, 0, mine_ref.at[s]).start()

        @pl.when(col > 0)
        def _():
            gather(s, col, 1, mine_ref.at[s]).start()

        own_part(s).start()

    def arrive(d, s):
        @pl.when(col >= d)
        def _():
            landed(part(s, col - d), ag_recv.at[s, col - d])

            @pl.when(col < last)
            def _():
                gather(s, col - d, 0, part(s, col - d)).start()

        @pl.when(col + d <= last)
        def _():
            landed(part(s, col + d), ag_recv.at[s, col + d])

            @pl.when(col > 0)
            def _():
                gather(s, col + d, 1, part(s, col + d)).start()

    def core_copy(p, k):
        return to(to_core.at[p % 2, k], from_core.at[p, k], core_send.at[p % 2, k], core_recv.at[p, k],
                  chip * CORES + 1 - core, col)

    def chip_copy(p, k):
        return to(to_chip.at[p % 2, k], from_chip.at[p, k], chip_send.at[p % 2, k], chip_recv.at[p, k],
                  chip_at(k) * CORES + core, col)

    def finish(p):
        total = to_chip[p % 2, CHIPS - 1].astype(F32)
        for k in range(CHIPS - 1):
            landed(from_chip.at[p, k], chip_recv.at[p, k])
            total = total + from_chip[p, k].astype(F32)
        block_y[p] = total.astype(BF)

    def col_copies(p, act):
        s, h = p % supers, p // supers
        pair = (half + h) % 2
        for j in range(2):
            w = pair * 2 + j
            src = block_y.at[p, pl.ds(j * width, width), :]
            remote = to(src, passed.at[s, col], col_send.at[p, j], col_recv.at[s, col], row, w)
            if act == "start":
                @pl.when(w != col)
                def _():
                    remote.start()

                @pl.when(w == col)
                def _():
                    pltpu.make_async_copy(src, passed.at[s, col], col_recv.at[s, col]).start()
            else:
                @pl.when(w != col)
                def _():
                    remote.wait_send()

    def row_copies(p, act):
        s, h = p % supers, p // supers
        pair = (half + h) % 2
        for j in range(2):
            c = pair * 2 + j
            dest = CORES * c + row // owners
            q = row % owners
            remote = to(passed.at[s, c], own_y.at[s, q], row_send.at[s, c], row_recv.at[s, q], dest, col)
            if act == "start":
                landed(passed.at[s, c], col_recv.at[s, c])

                @pl.when(dest != row)
                def _():
                    remote.start()

                @pl.when(dest == row)
                def _():
                    pltpu.make_async_copy(passed.at[s, c], own_y.at[s, q], row_recv.at[s, q]).start()
            else:
                @pl.when(dest != row)
                def _():
                    remote.wait_send()

    @pl.loop(0, passes)
    def _(p):
        s, h = p % supers, p // supers
        pair = (half + h) % 2

        @pl.when(h == 0)
        def _():
            landed(part(s, col), own_sem.at[s])
            arrive(1, s)

        @pl.when(h == 1)
        def _():
            arrive(2, s)
            arrive(3, s)

        @pl.when((p == 2) | (p == 3))
        def _():
            finish(p - 2)

        @pl.when(p >= 3)
        def _():
            finish(p - 1)

        @pl.when(p == passes - 1)
        def _():
            @pl.loop(0, passes - 1)
            def _(e):
                col_copies(e, "start")

        @pl.loop(0, CHIPS)
        def _(k):
            @pl.when(p >= 2)
            def _():
                core_copy(p - 2, k).wait_send()

                @pl.when(k < CHIPS - 1)
                def _():
                    chip_copy(p - 2, k).wait_send()

            landed(slab.at[0], slab_sem.at[0])
            slab_copy(k, 1, 1).start()
            to_core[p % 2, k] = jnp.dot(parts[s, pair], slab[0], preferred_element_type=F32).astype(BF)

            @pl.when(k > 0)
            def _():
                chip_copy(p, k - 1).start()

            landed(slab.at[1], slab_sem.at[1])

            @pl.when((k < CHIPS - 1) | (p < passes - 1))
            def _():
                slab_copy((k + 1) % CHIPS, 0, 0).start()

            core_copy(p, k).start()
            mine = jnp.dot(parts[s, pair], slab[1], preferred_element_type=F32)
            landed(from_core.at[p, k], core_recv.at[p, k])
            to_chip[p % 2, k] = (mine + from_core[p, k].astype(F32)).astype(BF)

    finish(passes - 1)

    @pl.loop(0, passes - 1)
    def _(e):
        row_copies(e, "start")

    col_copies(passes - 1, "start")
    row_copies(passes - 1, "start")

    partners = [
        chip * CORES + 1 - core,
        (y * SIDE + 1 - x) * CORES + core,
        ((1 - y) * SIDE + x) * CORES + core,
    ]
    stages = len(partners)

    def sum_copy(s, stage):
        return to(to_sum.at[s, stage], from_sum.at[s, stage], sum_send.at[s, stage], sum_recv.at[s, stage],
                  partners[stage], col)

    @pl.loop(0, supers)
    def _(s):
        t_ref[s] = jnp.zeros(t_ref.shape[1:], F32)
        for q in range(owners):
            landed(own_y.at[s, q], row_recv.at[s, q])
            here = own_y[s, q]
            y_ref[s, pl.ds(q * piece, piece), :] = here.astype(F32).T.astype(BF)
            for pr in range(2):
                rows = pl.ds(pr * 2 * width, 2 * width)
                t_ref[s, rows, :] += lax.dot_general(
                    parts[s, pr, :, pl.ds(q * piece, piece)], here, (((1,), (1,)), ((), ())),
                    preferred_element_type=F32,
                )
        to_sum[s, 0] = t_ref[s].astype(BF)

    for stage in range(stages):
        @pl.loop(0, supers)
        def _(s):
            sum_copy(s, stage).start()

        @pl.loop(0, supers)
        def _(s):
            landed(from_sum.at[s, stage], sum_recv.at[s, stage])
            total = to_sum[s, stage].astype(F32) + from_sum[s, stage].astype(F32)
            if stage < stages - 1:
                to_sum[s, stage + 1] = total.astype(BF)
            else:
                t_ref[s] = total

    @pl.loop(0, supers)
    def _(s):
        for stage in range(stages):
            sum_copy(s, stage).wait_send()

        @pl.loop(0, col_count)
        def _(w):
            @pl.when((w <= col) & (col < last))
            def _():
                gather(s, w, 0, part(s, w)).wait_send()

            @pl.when((w >= col) & (col > 0))
            def _():
                gather(s, w, 1, part(s, w)).wait_send()

    @pl.loop(0, passes)
    def _(p):
        col_copies(p, "wait")
        row_copies(p, "wait")

        @pl.when(p >= passes - 2)
        def _():
            @pl.loop(0, CHIPS)
            def _(k):
                core_copy(p, k).wait_send()

                @pl.when(k < CHIPS - 1)
                def _():
                    chip_copy(p, k).wait_send()


def fused(resident_inverse, factor, diag_inverse, anc_tiles, slot_tile):
    own_rows, own_cols = resident_inverse.shape
    supers, _, width = factor.shape
    row_count, col_count = lax.axis_size("row"), lax.axis_size("col")
    total_rows = own_rows * row_count
    row_mask = slot_rows(anc_tiles, slot_tile, total_rows // slot_tile.shape[0])
    own_mask = lax.dynamic_slice_in_dim(row_mask, lax.axis_index("row") * own_rows, own_rows, 1).astype(BF)
    mine = jnp.swapaxes(factor, 1, 2) * own_mask[:, None, :]
    piece = own_cols // row_count
    owners = row_count // CORES
    passes = 2 * supers
    wide = width * col_count
    dma = pltpu.SemaphoreType.DMA
    y, t = pl.pallas_call(
        lambda *refs: sweep(row_count, col_count, supers, *refs),
        out_shape=(
            jax.ShapeDtypeStruct((supers, own_rows, width), BF),
            jax.ShapeDtypeStruct((supers, wide, width), F32),
        ),
        in_specs=[pl.BlockSpec(memory_space=pl.ANY)] * 2,
        out_specs=[pl.BlockSpec(memory_space=pltpu.VMEM)] * 2,
        scratch_shapes=[
            pltpu.VMEM((2, own_rows, piece), BF),
            pltpu.VMEM((supers, 2, 2 * width, own_rows), BF),
            pltpu.VMEM((2, CHIPS, 2 * width, piece), BF),
            pltpu.VMEM((passes, CHIPS, 2 * width, piece), BF),
            pltpu.VMEM((2, CHIPS, 2 * width, piece), BF),
            pltpu.VMEM((passes, CHIPS - 1, 2 * width, piece), BF),
            pltpu.VMEM((passes, 2 * width, piece), BF),
            pltpu.VMEM((supers, col_count, width, piece), BF),
            pltpu.VMEM((supers, owners, width, piece), BF),
            pltpu.VMEM((supers, 3, wide, width), BF),
            pltpu.VMEM((supers, 3, wide, width), BF),
            dma((2,)), dma((supers,)),
            dma((2, supers, col_count)), dma((supers, col_count)),
            dma((2, CHIPS)), dma((passes, CHIPS)),
            dma((2, CHIPS)), dma((passes, CHIPS)),
            dma((passes, 2)), dma((supers, col_count)),
            dma((supers, col_count)), dma((supers, owners)),
            dma((supers, 3)), dma((supers, 3)),
        ],
        compiler_params=pltpu.CompilerParams(
            collective_id=0, has_side_effects=True, vmem_limit_bytes=67043328
        ),
    )(mine, resident_inverse)
    return (-(y * own_mask[:, :, None]), diag_inverse + t)


def on_device(*arrays):
    square = lax.axis_size("row") == CHIPS * CORES and lax.axis_size("col") == CHIPS
    return (fused if square else plain)(*arrays)


def solution(mesh):
    placed = (P("row", "col"), P(None, "row", "col"), P(None, None, "col"), P(), P())
    return jax.shard_map(
        on_device,
        mesh=mesh,
        in_specs=placed,
        out_specs=(P(None, "row", "col"), P(None, None, "col")),
        check_vma=False,
    )
```

```python
import jax
import jax.numpy as jnp
from jax import lax
from jax.experimental import pallas as pl
from jax.experimental.pallas import tpu as pltpu
from jax.sharding import PartitionSpec as P


def slot_rows(anc_tiles, slot_tile, tile_rows):
    listed = (anc_tiles[:, :, None] == slot_tile[None, None, :]).any(axis=1)
    return jnp.repeat(listed.astype(jnp.float32), tile_rows, axis=1)


def plain(resident_inverse, factor, diag_inverse, anc_tiles, slot_tile):
    own_rows, own_cols = resident_inverse.shape
    supers, _, part_width = factor.shape
    row_index = lax.axis_index("row")
    col_index = lax.axis_index("col")
    col_count = lax.axis_size("col")
    row_count = lax.axis_size("row")
    ratio = row_count // col_count
    owners = row_count // ratio
    total_rows = own_rows * row_count
    row_mask = slot_rows(anc_tiles, slot_tile, total_rows // slot_tile.shape[0])
    own_mask = lax.dynamic_slice_in_dim(row_mask, row_index * own_rows, own_rows, 1)
    mine = [factor[s] * own_mask[s].astype(jnp.bfloat16)[:, None] for s in range(supers)]
    last = col_count - 1
    up_moves = [(i, i + 1) for i in range(last)]
    down_moves = [(i + 1, i) for i in range(last)]
    chunk = own_cols // row_count

    parts = []
    for s in range(supers):
        ups, downs = [mine[s]], [mine[s]]
        for by in range(last):
            ups.append(lax.ppermute(ups[-1], "col", up_moves))
            downs.append(lax.ppermute(downs[-1], "col", down_moves))
        parts.append([mine[s]] + [ups[by] + downs[col_count - by] for by in range(1, col_count)])

    news, contribs = [], []
    for s in range(supers):
        wide = jnp.concatenate(parts[s], axis=1)
        partial = lax.dot_general(
            resident_inverse, wide, (((0,), (0,)), ((), ())), preferred_element_type=jnp.float32
        ).astype(jnp.bfloat16)
        summed = lax.psum_scatter(partial, "row", scatter_dimension=0, tiled=True)
        got = [summed[:, :part_width]]
        for by in range(1, col_count):
            piece = summed[:, by * part_width:(by + 1) * part_width]
            got.append(lax.ppermute(piece, "col", [(c, (c - by) % col_count) for c in range(col_count)]))
        got = jnp.stack(got)
        home = []
        for k in range(owners):
            block = (row_index + k) % owners
            piece = lax.dynamic_index_in_dim(got, (block - col_index) % col_count, 0, keepdims=False)
            moves = [(r, ratio * ((r + k) % owners) + r // owners) for r in range(row_count)]
            home.append(lax.ppermute(piece, "row", moves))
        home = jnp.stack(home)
        mine_y = jnp.concatenate([
            lax.dynamic_index_in_dim(home, (row_index // ratio - q) % owners, 0, keepdims=False)
            for q in range(owners)
        ], axis=0)
        news.append(-(mine_y * own_mask[s].astype(jnp.bfloat16)[:, None]))
        contribs.append(jnp.stack([
            jnp.einsum("rw,rv->wv", part, mine_y, preferred_element_type=jnp.float32)
            for part in parts[s]
        ]))
    stacked = jnp.stack(contribs, axis=1)
    ordered = jnp.stack([
        lax.dynamic_index_in_dim(stacked, (col_index - q) % col_count, 0, keepdims=False)
        for q in range(col_count)
    ], axis=1)
    totals = ordered.reshape(supers, col_count * part_width, part_width)
    step = 1
    while step < row_count:
        sent = totals.astype(jnp.bfloat16)
        got = lax.ppermute(sent, "row", [(i, i ^ step) for i in range(row_count)])
        totals = sent.astype(jnp.float32) + got.astype(jnp.float32)
        step *= 2
    return (jnp.stack(news), diag_inverse + totals)

MESH = pl.DeviceIdType.MESH
BF = jnp.bfloat16
F32 = jnp.float32
CORES = 2
SIDE = 2
CHIPS = SIDE * SIDE
DEPTH = 3


def sweep(row_count, col_count, supers, factor_ref, matrix_ref, mask_ref, y_out, t_out,
          y_ref, t_ref, slab, parts, to_core, from_core, to_chip, from_chip, bank, own_y, to_sum, from_sum, all_sum,
          slab_sem, own_sem, out_sem, ag_send, ag_recv, core_send, core_recv, chip_send, chip_recv,
          col_send, col_recv, row_send, row_recv, sum_send, sum_recv, all_send, all_recv, go):
    row = lax.axis_index("row")
    col = lax.axis_index("col")
    last = col_count - 1
    core = row % CORES
    chip = row // CORES
    x, y = chip % SIDE, chip // SIDE
    half = col // 2
    width = parts.shape[2]
    piece = slab.shape[2]
    owners = row_count // CORES
    passes = col_count * supers

    end = (col == 0) | (col == last)

    def plan(p):
        late = p // (2 * supers)
        e = p - 2 * supers
        tail = e // (2 * (supers - 1))
        order = (1 - tail) * (2 + e // (supers - 1)) + tail * (e - 2 * (supers - 2))
        which = (1 - tail) * (e % (supers - 1)) + tail * (supers - 1)
        return (1 - late) * (p // supers) + late * order, (1 - late) * (p % supers) + late * which

    def place(o):
        far, odd = o // 2, o % 2
        return (1 - far) * (col + odd * (1 - 2 * (col % 2))) + far * ((2 - half) + odd * (1 - 2 * half))

    barrier = pltpu.get_barrier_semaphore()

    @pl.loop(1, row_count)
    def _(by):
        pl.semaphore_signal(barrier, inc=1, device_id=((row + by) % row_count, col), device_id_type=MESH)

    @pl.loop(1, col_count)
    def _(by):
        pl.semaphore_signal(barrier, inc=1, device_id=(row, (col + by) % col_count), device_id_type=MESH)

    def to(src, dst, send, recv, r, c):
        return pltpu.make_async_remote_copy(
            src_ref=src, dst_ref=dst, send_sem=send, recv_sem=recv, device_id=(r, c), device_id_type=MESH
        )

    def landed(ref, sem):
        pltpu.make_async_copy(ref, ref, sem).wait()

    def part(s, w):
        return parts.at[s, w]

    def gather(s, w, way, src):
        return to(src, part(s, w), ag_send.at[way, s, w], ag_recv.at[s, w], row, col + (1 - 2 * way))

    def chip_at(k):
        xk = (x + 1 - k // 2) % 2
        yk = (y + 1 - k % 2) % 2
        return yk * SIDE + xk

    per_pass = 2 * CHIPS

    def slab_copy(step):
        j = step % per_pass
        end, begun = j // (per_pass - 1), (j + per_pass - 1) // per_pass
        even = 1 - j % 2
        own = end + (1 - end) * even * begun
        k = (1 - end) * ((1 - even) * ((j + 1) // 2) + even * (j // 2 - begun)) + end * (CHIPS - 1)
        which = chip_at(k) * CORES + (core + 1 - own) % CORES
        off = pl.multiple_of(which * piece, piece)
        slot = step % DEPTH
        return pltpu.make_async_copy(matrix_ref.at[:, pl.ds(off, piece)], slab.at[slot], slab_sem.at[slot])

    def next_slab(step):
        slot = step % DEPTH
        landed(slab.at[slot], slab_sem.at[slot])

        @pl.when(step + DEPTH - 1 < passes * per_pass)
        def _():
            slab_copy(step + DEPTH - 1).start()

        return slot

    def load(s):
        return pltpu.make_async_copy(factor_ref.at[s], y_ref.at[s], own_sem.at[s])

    @pl.loop(0, supers)
    def _(s):
        load(s).start()

    for step in range(DEPTH - 1):
        slab_copy(step).start()

    def own_part(s):
        landed(y_ref.at[s], own_sem.at[s])
        parts[s, col] = (y_ref[s].astype(F32).T * mask_ref[s]).astype(BF)

    def send_own(s):
        @pl.when(col < last)
        def _():
            gather(s, col, 0, part(s, col)).start()

        @pl.when(col > 0)
        def _():
            gather(s, col, 1, part(s, col)).start()

    own_part(0)
    pl.semaphore_wait(barrier, row_count - 1 + last)

    @pl.loop(1, supers)
    def _(s):
        send_own(s - 1)
        own_part(s)

    send_own(supers - 1)

    def arrive(d, s):
        @pl.when(col >= d)
        def _():
            landed(part(s, col - d), ag_recv.at[s, col - d])

        @pl.when(col + d <= last)
        def _():
            landed(part(s, col + d), ag_recv.at[s, col + d])

    def forward(d, s):
        @pl.when((col >= d) & (col < last))
        def _():
            gather(s, col - d, 0, part(s, col - d)).start()

        @pl.when((col + d <= last) & (col > 0))
        def _():
            gather(s, col + d, 1, part(s, col + d)).start()

    def core_copy(p, k):
        return to(to_core.at[p % 2, k], from_core.at[p, k], core_send.at[p % 2, k], core_recv.at[p, k],
                  chip * CORES + 1 - core, col)

    def chip_copy(p, k):
        return to(to_chip.at[p % 2, k], from_chip.at[p, k], chip_send.at[p % 2, k], chip_recv.at[p, k],
                  chip_at(k) * CORES + core, col)

    def finish(p):
        o, s = plan(p)
        total = to_chip[p % 2, CHIPS - 1].astype(F32)
        for k in range(CHIPS - 1):
            landed(from_chip.at[p, k], chip_recv.at[p, k])
            total = total + from_chip[p, k].astype(F32)
        bank[s, o] = total.astype(BF)

    def col_copy(s, o):
        return to(bank.at[s, o], bank.at[s, col_count + col], col_send.at[s, o], col_recv.at[s, col], row, place(o))

    def row_copy(s, o, act):
        c = place(o)
        dest = CORES * c + row // owners
        q = row % owners
        src = bank.at[s, ((o + col_count - 1) // col_count) * (col_count + c)]
        remote = to(src, own_y.at[s, q], row_send.at[s, o], row_recv.at[s, q], dest, col)
        if act == "start":
            @pl.when(o > 0)
            def _():
                landed(src, col_recv.at[s, c])

            @pl.when(dest != row)
            def _():
                remote.start()

            @pl.when(dest == row)
            def _():
                pltpu.make_async_copy(src, own_y.at[s, q], row_recv.at[s, q]).start()
        else:
            @pl.when(dest != row)
            def _():
                remote.wait_send()

    @pl.loop(0, passes)
    def _(p):
        o, s = plan(p)
        w = place(o)

        @pl.when(o > 0)
        def _():
            for d in range(1, col_count):
                @pl.when(o == d)
                def _():
                    arrive(d, s)

                    if d == 1:
                        @pl.when(s < supers - 1)
                        def _():
                            forward(1, s)
                    if d == 2:
                        forward(2, s)

                        @pl.when(s == supers - 2)
                        def _():
                            forward(1, supers - 1)

        @pl.when((p == passes - 1) & end)
        def _():
            for c in range(1, last):
                pl.semaphore_signal(go, inc=1, device_id=(row, c), device_id_type=MESH)

        @pl.when(p >= 2)
        def _():
            finish(p - 2)

        @pl.loop(0, CHIPS + 1)
        def _(k):
            @pl.when((k == 1) & (p >= 2))
            def _():
                before, which = plan(p - 2)

                @pl.when(before == 0)
                def _():
                    row_copy(which, 0, "start")

                @pl.when(((before == 1) & end) | (before == 2))
                def _():
                    col_copy(which, before).start()

            @pl.when((k == 1) & (p == passes - 1) & end)
            def _():
                @pl.loop(0, supers - 1)
                def _(e):
                    col_copy(e, 3).start()

            @pl.when(k < CHIPS)
            def _():
                @pl.when(p >= 2)
                def _():
                    core_copy(p - 2, k).wait_send()

                slot = next_slab(p * per_pass + 2 * k - (k + CHIPS - 1) // CHIPS)

                @pl.when(k == 1)
                def _():
                    core_copy(p, 0).start()

                to_core[p % 2, k] = jnp.dot(parts[s, w], slab[slot], preferred_element_type=F32).astype(BF)

                @pl.when(k >= 2)
                def _():
                    chip_copy(p, k - 2).start()

            @pl.when(k > 0)
            def _():
                slot = next_slab(p * per_pass + 2 * k - k // CHIPS)

                @pl.when(k < CHIPS)
                def _():
                    core_copy(p, k).start()

                @pl.when(k == CHIPS)
                def _():
                    chip_copy(p, CHIPS - 2).start()

                @pl.when((p >= 2) & (k < CHIPS))
                def _():
                    chip_copy(p - 2, k - 1).wait_send()

                mine = jnp.dot(parts[s, w], slab[slot], preferred_element_type=F32)
                landed(from_core.at[p, k - 1], core_recv.at[p, k - 1])
                to_chip[p % 2, k - 1] = (mine + from_core[p, k - 1].astype(F32)).astype(BF)

    def sum_copy(s, by):
        r = (row + by) % row_count
        return to(to_sum.at[s, r], from_sum.at[s, row], sum_send.at[s, r], sum_recv.at[s, row], r, col)

    def all_copy(s, by):
        r = (row + by) % row_count
        return to(all_sum.at[s, row], all_sum.at[s, row], all_send.at[s, r], all_recv.at[s, row], r, col)

    def out_copy(s):
        return pltpu.make_async_copy(y_ref.at[s], y_out.at[s], out_sem.at[0, s])

    def sum_out(s):
        return pltpu.make_async_copy(all_sum.at[s], t_out.at[s], out_sem.at[1, s])

    def settle(s):
        t_ref[...] = jnp.zeros(t_ref.shape, F32)
        for q in range(owners):
            landed(own_y.at[s, q], row_recv.at[s, q])
            here = own_y[s, q]
            off = q * piece
            mine = parts[s, :, :, pl.ds(off, piece)].reshape(t_ref.shape[0], piece)
            t_ref[...] += lax.dot_general(mine, here, (((1,), (1,)), ((), ())), preferred_element_type=F32)
        to_sum[s] = t_ref[...].reshape(to_sum.shape[1:]).astype(BF)
        for q in range(owners):
            off = q * piece
            y_ref[s, pl.ds(off, piece), :] = (
                own_y[s, q].astype(F32) * mask_ref[s, :, pl.ds(off, piece)]
            ).T.astype(BF)

        @pl.loop(1, row_count)
        def _(by):
            sum_copy(s, by).start()

        out_copy(s).start()

    def add_up(s):
        @pl.loop(1, row_count)
        def _(by):
            r = (row + by) % row_count
            landed(from_sum.at[s, r], sum_recv.at[s, r])

        from_sum[s, row] = to_sum[s, row]
        total = from_sum[s, 0].astype(F32)
        for r in range(1, row_count):
            total = total + from_sum[s, r].astype(F32)
        all_sum[s, row] = total.astype(BF)

        @pl.loop(1, row_count)
        def _(by):
            all_copy(s, by).start()

    def collect(s):
        @pl.loop(1, row_count)
        def _(by):
            r = (row + by) % row_count
            landed(all_sum.at[s, r], all_recv.at[s, r])

        sum_out(s).start()

    finish(passes - 2)

    @pl.when(end)
    def _():
        col_copy(supers - 1, 2).start()

    finish(passes - 1)

    @pl.when(end)
    def _():
        col_copy(supers - 1, 3).start()

    @pl.when(jnp.logical_not(end))
    def _():
        col_copy(supers - 1, 2).start()

    @pl.loop(0, supers)
    def _(s):
        row_copy(s, 1, "start")

    @pl.loop(0, 2 * (supers - 1))
    def _(i):
        row_copy(i // 2, 2 + i % 2, "start")

    @pl.when(jnp.logical_not(end))
    def _():
        pl.semaphore_wait(go, 2)

        @pl.loop(0, 2 * supers)
        def _(i):
            col_copy(i % supers, 1 + 2 * (i // supers)).start()

    settle(0)
    for o in (2, 3):
        row_copy(supers - 1, o, "start")

    @pl.loop(1, supers - 1)
    def _(s):
        settle(s)

    @pl.loop(0, supers - 1)
    def _(s):
        add_up(s)

    settle(supers - 1)

    @pl.loop(0, supers - 1)
    def _(s):
        collect(s)

    add_up(supers - 1)
    collect(supers - 1)

    @pl.loop(0, supers)
    def _(s):
        out_copy(s).wait()
        sum_out(s).wait()

        @pl.loop(1, row_count)
        def _(by):
            sum_copy(s, by).wait_send()
            all_copy(s, by).wait_send()

        @pl.loop(0, col_count)
        def _(w):
            @pl.when((w <= col) & (col < last))
            def _():
                gather(s, w, 0, part(s, w)).wait_send()

            @pl.when((w >= col) & (col > 0))
            def _():
                gather(s, w, 1, part(s, w)).wait_send()

    @pl.loop(0, passes)
    def _(p):
        s, o = p // col_count, p % col_count
        row_copy(s, o, "wait")

        @pl.when(o > 0)
        def _():
            col_copy(s, o).wait_send()

        @pl.when(p >= passes - 2)
        def _():
            @pl.loop(0, CHIPS)
            def _(k):
                core_copy(p, k).wait_send()

                @pl.when(k < CHIPS - 1)
                def _():
                    chip_copy(p, k).wait_send()


def fused(resident_inverse, factor, diag_inverse, anc_tiles, slot_tile):
    own_rows, own_cols = resident_inverse.shape
    supers, _, width = factor.shape
    row_count, col_count = lax.axis_size("row"), lax.axis_size("col")
    total_rows = own_rows * row_count
    row_mask = slot_rows(anc_tiles, slot_tile, total_rows // slot_tile.shape[0])
    own_mask = lax.dynamic_slice_in_dim(row_mask, lax.axis_index("row") * own_rows, own_rows, 1)
    piece = own_cols // row_count
    owners = row_count // CORES
    passes = col_count * supers
    wide = width * col_count
    dma = pltpu.SemaphoreType.DMA
    y, t = pl.pallas_call(
        lambda *refs: sweep(row_count, col_count, supers, *refs),
        out_shape=(
            jax.ShapeDtypeStruct((supers, own_rows, width), BF),
            jax.ShapeDtypeStruct((supers, row_count, wide // row_count, width), BF),
        ),
        in_specs=[pl.BlockSpec(memory_space=pl.ANY)] * 2 + [pl.BlockSpec(memory_space=pltpu.VMEM)],
        out_specs=[pl.BlockSpec(memory_space=pl.ANY)] * 2,
        scratch_shapes=[
            pltpu.VMEM((supers, own_rows, width), BF),
            pltpu.VMEM((wide, width), F32),
            pltpu.VMEM((DEPTH, own_rows, piece), BF),
            pltpu.VMEM((supers, col_count, width, own_rows), BF),
            pltpu.VMEM((2, CHIPS, width, piece), BF),
            pltpu.VMEM((passes, CHIPS, width, piece), BF),
            pltpu.VMEM((2, CHIPS, width, piece), BF),
            pltpu.VMEM((passes, CHIPS - 1, width, piece), BF),
            pltpu.VMEM((supers, 2 * col_count, width, piece), BF),
            pltpu.VMEM((supers, owners, width, piece), BF),
            pltpu.VMEM((supers, row_count, wide // row_count, width), BF),
            pltpu.VMEM((supers, row_count, wide // row_count, width), BF),
            pltpu.VMEM((supers, row_count, wide // row_count, width), BF),
            dma((DEPTH,)), dma((supers,)), dma((2, supers)),
            dma((2, supers, col_count)), dma((supers, col_count)),
            dma((2, CHIPS)), dma((passes, CHIPS)),
            dma((2, CHIPS)), dma((passes, CHIPS)),
            dma((supers, col_count)), dma((supers, col_count)),
            dma((supers, col_count)), dma((supers, owners)),
            dma((supers, row_count)), dma((supers, row_count)),
            dma((supers, row_count)), dma((supers, row_count)),
            pltpu.SemaphoreType.REGULAR,
        ],
        compiler_params=pltpu.CompilerParams(
            collective_id=0, has_side_effects=True, vmem_limit_bytes=67043328
        ),
    )(factor, resident_inverse, own_mask[:, None, :])
    return (-y, diag_inverse + t.reshape(diag_inverse.shape).astype(F32))


def on_device(*arrays):
    square = lax.axis_size("row") == CHIPS * CORES and lax.axis_size("col") == CHIPS
    return (fused if square else plain)(*arrays)


def solution(mesh):
    placed = (P("row", "col"), P(None, "row", "col"), P(None, None, "col"), P(), P())
    return jax.shard_map(
        on_device,
        mesh=mesh,
        in_specs=placed,
        out_specs=(P(None, "row", "col"), P(None, None, "col")),
        check_vma=False,
    )
```

```python
import jax
import jax.numpy as jnp
from jax import lax
from jax.experimental import pallas as pl
from jax.experimental.pallas import tpu as pltpu
from jax.sharding import PartitionSpec as P


def slot_rows(anc_tiles, slot_tile, tile_rows):
    listed = (anc_tiles[:, :, None] == slot_tile[None, None, :]).any(axis=1)
    return jnp.repeat(listed.astype(jnp.float32), tile_rows, axis=1)


def plain(resident_inverse, factor, diag_inverse, anc_tiles, slot_tile):
    own_rows, own_cols = resident_inverse.shape
    supers, _, part_width = factor.shape
    row_index = lax.axis_index("row")
    col_index = lax.axis_index("col")
    col_count = lax.axis_size("col")
    row_count = lax.axis_size("row")
    ratio = row_count // col_count
    owners = row_count // ratio
    total_rows = own_rows * row_count
    row_mask = slot_rows(anc_tiles, slot_tile, total_rows // slot_tile.shape[0])
    own_mask = lax.dynamic_slice_in_dim(row_mask, row_index * own_rows, own_rows, 1)
    mine = [factor[s] * own_mask[s].astype(jnp.bfloat16)[:, None] for s in range(supers)]
    last = col_count - 1
    up_moves = [(i, i + 1) for i in range(last)]
    down_moves = [(i + 1, i) for i in range(last)]
    chunk = own_cols // row_count

    parts = []
    for s in range(supers):
        ups, downs = [mine[s]], [mine[s]]
        for by in range(last):
            ups.append(lax.ppermute(ups[-1], "col", up_moves))
            downs.append(lax.ppermute(downs[-1], "col", down_moves))
        parts.append([mine[s]] + [ups[by] + downs[col_count - by] for by in range(1, col_count)])

    news, contribs = [], []
    for s in range(supers):
        wide = jnp.concatenate(parts[s], axis=1)
        partial = lax.dot_general(
            resident_inverse, wide, (((0,), (0,)), ((), ())), preferred_element_type=jnp.float32
        ).astype(jnp.bfloat16)
        summed = lax.psum_scatter(partial, "row", scatter_dimension=0, tiled=True)
        got = [summed[:, :part_width]]
        for by in range(1, col_count):
            piece = summed[:, by * part_width:(by + 1) * part_width]
            got.append(lax.ppermute(piece, "col", [(c, (c - by) % col_count) for c in range(col_count)]))
        got = jnp.stack(got)
        home = []
        for k in range(owners):
            block = (row_index + k) % owners
            piece = lax.dynamic_index_in_dim(got, (block - col_index) % col_count, 0, keepdims=False)
            moves = [(r, ratio * ((r + k) % owners) + r // owners) for r in range(row_count)]
            home.append(lax.ppermute(piece, "row", moves))
        home = jnp.stack(home)
        mine_y = jnp.concatenate([
            lax.dynamic_index_in_dim(home, (row_index // ratio - q) % owners, 0, keepdims=False)
            for q in range(owners)
        ], axis=0)
        news.append(-(mine_y * own_mask[s].astype(jnp.bfloat16)[:, None]))
        contribs.append(jnp.stack([
            jnp.einsum("rw,rv->wv", part, mine_y, preferred_element_type=jnp.float32)
            for part in parts[s]
        ]))
    stacked = jnp.stack(contribs, axis=1)
    ordered = jnp.stack([
        lax.dynamic_index_in_dim(stacked, (col_index - q) % col_count, 0, keepdims=False)
        for q in range(col_count)
    ], axis=1)
    totals = ordered.reshape(supers, col_count * part_width, part_width)
    step = 1
    while step < row_count:
        sent = totals.astype(jnp.bfloat16)
        got = lax.ppermute(sent, "row", [(i, i ^ step) for i in range(row_count)])
        totals = sent.astype(jnp.float32) + got.astype(jnp.float32)
        step *= 2
    return (jnp.stack(news), diag_inverse + totals)

MESH = pl.DeviceIdType.MESH
BF = jnp.bfloat16
F32 = jnp.float32
CORES = 2
SIDE = 2
CHIPS = SIDE * SIDE
DEPTH = 3


def sweep(row_count, col_count, supers, factor_ref, matrix_ref, mask_ref, y_out, t_out,
          y_ref, t_ref, slab, parts, to_core, from_core, to_chip, from_chip, bank, own_y, to_sum, from_sum, all_sum,
          slab_sem, own_sem, out_sem, ag_send, ag_recv, core_send, core_recv, chip_send, chip_recv,
          col_send, col_recv, row_send, row_recv, sum_send, sum_recv, all_send, all_recv, go):
    row = lax.axis_index("row")
    col = lax.axis_index("col")
    last = col_count - 1
    core = row % CORES
    chip = row // CORES
    x, y = chip % SIDE, chip // SIDE
    half = col // 2
    width = parts.shape[2]
    piece = slab.shape[2]
    owners = row_count // CORES
    passes = col_count * supers

    end = (col == 0) | (col == last)

    def plan(p):
        late = p // (2 * supers)
        e = p - 2 * supers
        tail = e // (2 * (supers - 1))
        order = (1 - tail) * (2 + e // (supers - 1)) + tail * (e - 2 * (supers - 2))
        which = (1 - tail) * (e % (supers - 1)) + tail * (supers - 1)
        return (1 - late) * (p // supers) + late * order, (1 - late) * (p % supers) + late * which

    def place(o):
        far, odd = o // 2, o % 2
        return (1 - far) * (col + odd * (1 - 2 * (col % 2))) + far * ((2 - half) + odd * (1 - 2 * half))

    barrier = pltpu.get_barrier_semaphore()

    @pl.loop(1, row_count)
    def _(by):
        pl.semaphore_signal(barrier, inc=1, device_id=((row + by) % row_count, col), device_id_type=MESH)

    @pl.loop(1, col_count)
    def _(by):
        pl.semaphore_signal(barrier, inc=1, device_id=(row, (col + by) % col_count), device_id_type=MESH)

    def to(src, dst, send, recv, r, c):
        return pltpu.make_async_remote_copy(
            src_ref=src, dst_ref=dst, send_sem=send, recv_sem=recv, device_id=(r, c), device_id_type=MESH
        )

    def landed(ref, sem):
        pltpu.make_async_copy(ref, ref, sem).wait()

    def part(s, w):
        return parts.at[s, w]

    def gather(s, w, way, src):
        return to(src, part(s, w), ag_send.at[way, s, w], ag_recv.at[s, w], row, col + (1 - 2 * way))

    def chip_at(k):
        xk = (x + 1 - k // 2) % 2
        yk = (y + 1 - k % 2) % 2
        return yk * SIDE + xk

    per_pass = 2 * CHIPS

    def slab_copy(step):
        j = step % per_pass
        end, begun = j // (per_pass - 1), (j + per_pass - 1) // per_pass
        even = 1 - j % 2
        own = end + (1 - end) * even * begun
        k = (1 - end) * ((1 - even) * ((j + 1) // 2) + even * (j // 2 - begun)) + end * (CHIPS - 1)
        which = chip_at(k) * CORES + (core + 1 - own) % CORES
        off = pl.multiple_of(which * piece, piece)
        slot = step % DEPTH
        return pltpu.make_async_copy(matrix_ref.at[:, pl.ds(off, piece)], slab.at[slot], slab_sem.at[slot])

    def next_slab(step):
        slot = step % DEPTH
        landed(slab.at[slot], slab_sem.at[slot])

        @pl.when(step + DEPTH - 1 < passes * per_pass)
        def _():
            slab_copy(step + DEPTH - 1).start()

        return slot

    def load(s):
        return pltpu.make_async_copy(factor_ref.at[s], y_ref.at[s], own_sem.at[s])

    @pl.loop(0, supers)
    def _(s):
        load(s).start()

    for step in range(DEPTH - 1):
        slab_copy(step).start()

    def own_part(s):
        landed(y_ref.at[s], own_sem.at[s])
        parts[s, col] = (y_ref[s].astype(F32).T * mask_ref[s]).astype(BF)

    def send_own(s):
        @pl.when(col < last)
        def _():
            gather(s, col, 0, part(s, col)).start()

        @pl.when(col > 0)
        def _():
            gather(s, col, 1, part(s, col)).start()

    own_part(0)
    pl.semaphore_wait(barrier, row_count - 1 + last)

    @pl.loop(1, supers)
    def _(s):
        send_own(s - 1)
        own_part(s)

    send_own(supers - 1)

    def arrive(d, s):
        @pl.when(col >= d)
        def _():
            landed(part(s, col - d), ag_recv.at[s, col - d])

        @pl.when(col + d <= last)
        def _():
            landed(part(s, col + d), ag_recv.at[s, col + d])

    def forward(d, s):
        @pl.when((col >= d) & (col < last))
        def _():
            gather(s, col - d, 0, part(s, col - d)).start()

        @pl.when((col + d <= last) & (col > 0))
        def _():
            gather(s, col + d, 1, part(s, col + d)).start()

    def core_copy(p, k):
        return to(to_core.at[p % 2, k], from_core.at[p, k], core_send.at[p % 2, k], core_recv.at[p, k],
                  chip * CORES + 1 - core, col)

    def chip_copy(p, k):
        return to(to_chip.at[p % 2, k], from_chip.at[p, k], chip_send.at[p % 2, k], chip_recv.at[p, k],
                  chip_at(k) * CORES + core, col)

    def finish(p):
        o, s = plan(p)
        total = to_chip[p % 2, CHIPS - 1].astype(F32)
        for k in range(CHIPS - 1):
            landed(from_chip.at[p, k], chip_recv.at[p, k])
            total = total + from_chip[p, k].astype(F32)
        bank[s, o] = total.astype(BF)

    def col_copy(s, o):
        return to(bank.at[s, o], bank.at[s, col_count + col], col_send.at[s, o], col_recv.at[s, col], row, place(o))

    def row_copy(s, o, act):
        c = place(o)
        dest = CORES * c + row // owners
        q = row % owners
        src = bank.at[s, ((o + col_count - 1) // col_count) * (col_count + c)]
        remote = to(src, own_y.at[s, q], row_send.at[s, o], row_recv.at[s, q], dest, col)
        if act == "start":
            @pl.when(o > 0)
            def _():
                landed(src, col_recv.at[s, c])

            @pl.when(dest != row)
            def _():
                remote.start()

            @pl.when(dest == row)
            def _():
                pltpu.make_async_copy(src, own_y.at[s, q], row_recv.at[s, q]).start()
        else:
            @pl.when(dest != row)
            def _():
                remote.wait_send()

    @pl.loop(0, passes)
    def _(p):
        o, s = plan(p)
        w = place(o)

        @pl.when((p == passes - 1) & end)
        def _():
            row_copy(supers - 1, 1, "start")
            row_copy(0, 2, "start")
            row_copy(0, 3, "start")

        @pl.when(o > 0)
        def _():
            for d in range(1, col_count):
                @pl.when(o == d)
                def _():
                    arrive(d, s)

                    if d == 1:
                        @pl.when(s < supers - 1)
                        def _():
                            forward(1, s)
                    if d == 2:
                        forward(2, s)

                        @pl.when(s == supers - 2)
                        def _():
                            forward(1, supers - 1)

        @pl.when((p == passes - 1) & end)
        def _():
            for c in range(1, last):
                pl.semaphore_signal(go, inc=1, device_id=(row, c), device_id_type=MESH)

        @pl.when(p >= 2)
        def _():
            finish(p - 2)

        @pl.loop(0, CHIPS + 1)
        def _(k):
            @pl.when((k == 1) & (p >= 2))
            def _():
                before, which = plan(p - 2)

                @pl.when(before == 0)
                def _():
                    row_copy(which, 0, "start")

                @pl.when((before == 1) | (before == 2) | ((before == 3) & (which == 0)))
                def _():
                    col_copy(which, before).start()

            @pl.when((k == 2) & (p >= passes - 1 - supers) & (p < passes - 2) & end)
            def _():
                row_copy(p - (passes - 1 - supers), 1, "start")

            @pl.when((k == 1) & (p == passes - 1) & end)
            def _():
                @pl.loop(1, supers - 1)
                def _(e):
                    col_copy(e, 3).start()

            @pl.when(k < CHIPS)
            def _():
                @pl.when(p >= 2)
                def _():
                    core_copy(p - 2, k).wait_send()

                slot = next_slab(p * per_pass + 2 * k - (k + CHIPS - 1) // CHIPS)

                @pl.when(k == 1)
                def _():
                    core_copy(p, 0).start()

                to_core[p % 2, k] = jnp.dot(parts[s, w], slab[slot], preferred_element_type=F32).astype(BF)

                @pl.when(k >= 2)
                def _():
                    chip_copy(p, k - 2).start()

            @pl.when(k > 0)
            def _():
                slot = next_slab(p * per_pass + 2 * k - k // CHIPS)

                @pl.when(k < CHIPS)
                def _():
                    core_copy(p, k).start()

                @pl.when(k == CHIPS)
                def _():
                    chip_copy(p, CHIPS - 2).start()

                @pl.when((p >= 2) & (k < CHIPS))
                def _():
                    chip_copy(p - 2, k - 1).wait_send()

                mine = jnp.dot(parts[s, w], slab[slot], preferred_element_type=F32)
                landed(from_core.at[p, k - 1], core_recv.at[p, k - 1])
                to_chip[p % 2, k - 1] = (mine + from_core[p, k - 1].astype(F32)).astype(BF)

    def sum_copy(s, by):
        r = (row + by) % row_count
        return to(to_sum.at[s, r], from_sum.at[s, row], sum_send.at[s, r], sum_recv.at[s, row], r, col)

    def all_copy(s, by):
        r = (row + by) % row_count
        return to(all_sum.at[s, row], all_sum.at[s, row], all_send.at[s, r], all_recv.at[s, row], r, col)

    def out_copy(s):
        return pltpu.make_async_copy(y_ref.at[s], y_out.at[s], out_sem.at[0, s])

    def sum_out(s):
        return pltpu.make_async_copy(all_sum.at[s], t_out.at[s], out_sem.at[1, s])

    def settle(s):
        t_ref[...] = jnp.zeros(t_ref.shape, F32)
        for q in range(owners):
            landed(own_y.at[s, q], row_recv.at[s, q])
            here = own_y[s, q]
            off = q * piece
            mine = parts[s, :, :, pl.ds(off, piece)].reshape(t_ref.shape[0], piece)
            t_ref[...] += lax.dot_general(mine, here, (((1,), (1,)), ((), ())), preferred_element_type=F32)
        to_sum[s] = t_ref[...].reshape(to_sum.shape[1:]).astype(BF)
        for q in range(owners):
            off = q * piece
            y_ref[s, pl.ds(off, piece), :] = (
                own_y[s, q].astype(F32) * -mask_ref[s, :, pl.ds(off, piece)]
            ).T.astype(BF)

        @pl.loop(1, row_count)
        def _(by):
            sum_copy(s, by).start()

        out_copy(s).start()

    def add_up(s):
        @pl.loop(1, row_count)
        def _(by):
            r = (row + by) % row_count
            landed(from_sum.at[s, r], sum_recv.at[s, r])

        from_sum[s, row] = to_sum[s, row]
        total = from_sum[s, 0].astype(F32)
        for r in range(1, row_count):
            total = total + from_sum[s, r].astype(F32)
        all_sum[s, row] = total.astype(BF)

        @pl.loop(1, row_count)
        def _(by):
            all_copy(s, by).start()

    def collect(s):
        @pl.loop(1, row_count)
        def _(by):
            r = (row + by) % row_count
            landed(all_sum.at[s, r], all_recv.at[s, r])

        sum_out(s).start()

    def drain_early():
        @pl.loop(0, supers)
        def _(s):
            @pl.loop(0, col_count)
            def _(w):
                @pl.when((w <= col) & (col < last))
                def _():
                    gather(s, w, 0, part(s, w)).wait_send()

                @pl.when((w >= col) & (col > 0))
                def _():
                    gather(s, w, 1, part(s, w)).wait_send()

        @pl.loop(passes - 2, passes)
        def _(p):
            @pl.loop(0, CHIPS)
            def _(k):
                core_copy(p, k).wait_send()

                @pl.when(k < CHIPS - 1)
                def _():
                    chip_copy(p, k).wait_send()

    def drain(s):
        @pl.loop(0, col_count)
        def _(o):
            row_copy(s, o, "wait")

            @pl.when(o > 0)
            def _():
                col_copy(s, o).wait_send()

        @pl.loop(1, row_count)
        def _(by):
            sum_copy(s, by).wait_send()

        out_copy(s).wait()

    finish(passes - 2)

    def middle_rows():
        @pl.loop(2, 2 * (supers - 1))
        def _(i):
            row_copy(i // 2, 2 + i % 2, "start")

    @pl.when(end)
    def _():
        col_copy(supers - 1, 2).start()
        middle_rows()

    finish(passes - 1)

    @pl.when(end)
    def _():
        col_copy(supers - 1, 3).start()

    @pl.when(jnp.logical_not(end))
    def _():
        col_copy(supers - 1, 2).start()

        @pl.loop(0, supers)
        def _(s):
            row_copy(s, 1, "start")

        row_copy(0, 2, "start")
        row_copy(0, 3, "start")
        middle_rows()

    drain_early()

    @pl.when(jnp.logical_not(end))
    def _():
        pl.semaphore_wait(go, 2)

        @pl.loop(1, supers)
        def _(s):
            col_copy(s, 3).start()

    settle(0)
    for o in (2, 3):
        row_copy(supers - 1, o, "start")

    @pl.loop(1, supers)
    def _(s):
        settle(s)

    @pl.loop(0, supers - 1)
    def _(s):
        add_up(s)

    add_up(supers - 1)

    @pl.loop(0, supers - 1)
    def _(s):
        collect(s)

    @pl.loop(0, supers)
    def _(s):
        drain(s)

    collect(supers - 1)

    @pl.loop(0, supers)
    def _(s):
        @pl.loop(1, row_count)
        def _(by):
            all_copy(s, by).wait_send()

        sum_out(s).wait()


def close(y_ref, t_ref, diag_ref, new_ref, out_ref, y, t, diag, y_sem, t_sem, diag_sem, new_sem, out_sem):
    supers = y_ref.shape[0]

    def copy(src, dst, sem):
        return pltpu.make_async_copy(src, dst, sem)

    t_in, diag_in = copy(t_ref, t, t_sem), copy(diag_ref, diag, diag_sem)
    y_in = [copy(y_ref.at[s], y.at[s], y_sem.at[s]) for s in range(supers)]
    y_over = [copy(y.at[s], new_ref.at[s], new_sem.at[s]) for s in range(supers)]
    for each in y_in + [t_in, diag_in]:
        each.start()
    for s in range(supers):
        y_in[s].wait()
        y_over[s].start()
    t_in.wait()
    diag_in.wait()
    diag[...] += t[...].astype(F32)
    over = copy(diag, out_ref, out_sem)
    over.start()
    for each in y_over + [over]:
        each.wait()


def fused(resident_inverse, factor, diag_inverse, anc_tiles, slot_tile):
    own_rows, own_cols = resident_inverse.shape
    supers, _, width = factor.shape
    row_count, col_count = lax.axis_size("row"), lax.axis_size("col")
    total_rows = own_rows * row_count
    row_mask = slot_rows(anc_tiles, slot_tile, total_rows // slot_tile.shape[0])
    own_mask = lax.dynamic_slice_in_dim(row_mask, lax.axis_index("row") * own_rows, own_rows, 1)
    piece = own_cols // row_count
    owners = row_count // CORES
    passes = col_count * supers
    wide = width * col_count
    dma = pltpu.SemaphoreType.DMA
    y, t = pl.pallas_call(
        lambda *refs: sweep(row_count, col_count, supers, *refs),
        out_shape=(
            jax.ShapeDtypeStruct((supers, own_rows, width), BF),
            jax.ShapeDtypeStruct((supers, row_count, wide // row_count, width), BF),
        ),
        in_specs=[pl.BlockSpec(memory_space=pl.ANY)] * 2 + [pl.BlockSpec(memory_space=pltpu.VMEM)],
        out_specs=[pl.BlockSpec(memory_space=pl.ANY)] * 2,
        scratch_shapes=[
            pltpu.VMEM((supers, own_rows, width), BF),
            pltpu.VMEM((wide, width), F32),
            pltpu.VMEM((DEPTH, own_rows, piece), BF),
            pltpu.VMEM((supers, col_count, width, own_rows), BF),
            pltpu.VMEM((2, CHIPS, width, piece), BF),
            pltpu.VMEM((passes, CHIPS, width, piece), BF),
            pltpu.VMEM((2, CHIPS, width, piece), BF),
            pltpu.VMEM((passes, CHIPS - 1, width, piece), BF),
            pltpu.VMEM((supers, 2 * col_count, width, piece), BF),
            pltpu.VMEM((supers, owners, width, piece), BF),
            pltpu.VMEM((supers, row_count, wide // row_count, width), BF),
            pltpu.VMEM((supers, row_count, wide // row_count, width), BF),
            pltpu.VMEM((supers, row_count, wide // row_count, width), BF),
            dma((DEPTH,)), dma((supers,)), dma((2, supers)),
            dma((2, supers, col_count)), dma((supers, col_count)),
            dma((2, CHIPS)), dma((passes, CHIPS)),
            dma((2, CHIPS)), dma((passes, CHIPS)),
            dma((supers, col_count)), dma((supers, col_count)),
            dma((supers, col_count)), dma((supers, owners)),
            dma((supers, row_count)), dma((supers, row_count)),
            dma((supers, row_count)), dma((supers, row_count)),
            pltpu.SemaphoreType.REGULAR,
        ],
        compiler_params=pltpu.CompilerParams(
            collective_id=0, has_side_effects=True, vmem_limit_bytes=67043328
        ),
    )(factor, resident_inverse, own_mask[:, None, :])
    t = t.reshape(diag_inverse.shape)
    return tuple(pl.pallas_call(
        close,
        in_specs=[pl.BlockSpec(memory_space=pl.ANY)] * 3,
        out_specs=[pl.BlockSpec(memory_space=pl.ANY)] * 2,
        out_shape=(jax.ShapeDtypeStruct(y.shape, BF), jax.ShapeDtypeStruct(t.shape, F32)),
        scratch_shapes=[
            pltpu.VMEM(y.shape, BF), pltpu.VMEM(t.shape, BF), pltpu.VMEM(t.shape, F32),
            dma((supers,)), dma(()), dma(()), dma((supers,)), dma(()),
        ],
    )(y, t, diag_inverse))


def on_device(*arrays):
    square = lax.axis_size("row") == CHIPS * CORES and lax.axis_size("col") == CHIPS
    return (fused if square else plain)(*arrays)


def solution(mesh):
    placed = (P("row", "col"), P(None, "row", "col"), P(None, None, "col"), P(), P())
    return jax.shard_map(
        on_device,
        mesh=mesh,
        in_specs=placed,
        out_specs=(P(None, "row", "col"), P(None, None, "col")),
        check_vma=False,
    )
```

```python
import jax
import jax.numpy as jnp
from jax import lax
from jax.experimental import pallas as pl
from jax.experimental.pallas import tpu as pltpu
from jax.sharding import PartitionSpec as P


def slot_rows(anc_tiles, slot_tile, tile_rows):
    listed = (anc_tiles[:, :, None] == slot_tile[None, None, :]).any(axis=1)
    return jnp.repeat(listed.astype(jnp.float32), tile_rows, axis=1)


def plain(resident_inverse, factor, diag_inverse, anc_tiles, slot_tile):
    own_rows, own_cols = resident_inverse.shape
    supers, _, part_width = factor.shape
    row_index = lax.axis_index("row")
    col_index = lax.axis_index("col")
    col_count = lax.axis_size("col")
    row_count = lax.axis_size("row")
    ratio = row_count // col_count
    owners = row_count // ratio
    total_rows = own_rows * row_count
    row_mask = slot_rows(anc_tiles, slot_tile, total_rows // slot_tile.shape[0])
    own_mask = lax.dynamic_slice_in_dim(row_mask, row_index * own_rows, own_rows, 1)
    mine = [factor[s] * own_mask[s].astype(jnp.bfloat16)[:, None] for s in range(supers)]
    last = col_count - 1
    up_moves = [(i, i + 1) for i in range(last)]
    down_moves = [(i + 1, i) for i in range(last)]
    chunk = own_cols // row_count

    parts = []
    for s in range(supers):
        ups, downs = [mine[s]], [mine[s]]
        for by in range(last):
            ups.append(lax.ppermute(ups[-1], "col", up_moves))
            downs.append(lax.ppermute(downs[-1], "col", down_moves))
        parts.append([mine[s]] + [ups[by] + downs[col_count - by] for by in range(1, col_count)])

    news, contribs = [], []
    for s in range(supers):
        wide = jnp.concatenate(parts[s], axis=1)
        partial = lax.dot_general(
            resident_inverse, wide, (((0,), (0,)), ((), ())), preferred_element_type=jnp.float32
        ).astype(jnp.bfloat16)
        summed = lax.psum_scatter(partial, "row", scatter_dimension=0, tiled=True)
        got = [summed[:, :part_width]]
        for by in range(1, col_count):
            piece = summed[:, by * part_width:(by + 1) * part_width]
            got.append(lax.ppermute(piece, "col", [(c, (c - by) % col_count) for c in range(col_count)]))
        got = jnp.stack(got)
        home = []
        for k in range(owners):
            block = (row_index + k) % owners
            piece = lax.dynamic_index_in_dim(got, (block - col_index) % col_count, 0, keepdims=False)
            moves = [(r, ratio * ((r + k) % owners) + r // owners) for r in range(row_count)]
            home.append(lax.ppermute(piece, "row", moves))
        home = jnp.stack(home)
        mine_y = jnp.concatenate([
            lax.dynamic_index_in_dim(home, (row_index // ratio - q) % owners, 0, keepdims=False)
            for q in range(owners)
        ], axis=0)
        news.append(-(mine_y * own_mask[s].astype(jnp.bfloat16)[:, None]))
        contribs.append(jnp.stack([
            jnp.einsum("rw,rv->wv", part, mine_y, preferred_element_type=jnp.float32)
            for part in parts[s]
        ]))
    stacked = jnp.stack(contribs, axis=1)
    ordered = jnp.stack([
        lax.dynamic_index_in_dim(stacked, (col_index - q) % col_count, 0, keepdims=False)
        for q in range(col_count)
    ], axis=1)
    totals = ordered.reshape(supers, col_count * part_width, part_width)
    step = 1
    while step < row_count:
        sent = totals.astype(jnp.bfloat16)
        got = lax.ppermute(sent, "row", [(i, i ^ step) for i in range(row_count)])
        totals = sent.astype(jnp.float32) + got.astype(jnp.float32)
        step *= 2
    return (jnp.stack(news), diag_inverse + totals)

MESH = pl.DeviceIdType.MESH
BF = jnp.bfloat16
F32 = jnp.float32
CORES = 2
SIDE = 2
CHIPS = SIDE * SIDE
DEPTH = 4


def sweep(row_count, col_count, supers, factor_ref, matrix_ref, mask_ref, y_out, t_out,
          y_ref, t_ref, slab, parts, to_core, from_core, to_chip, from_chip, bank, own_y, to_sum, from_sum, all_sum,
          slab_sem, own_sem, out_sem, ag_send, ag_recv, core_send, core_recv, chip_send, chip_recv,
          col_send, col_recv, row_send, row_recv, sum_send, sum_recv, all_send, all_recv, go):
    row = lax.axis_index("row")
    col = lax.axis_index("col")
    last = col_count - 1
    core = row % CORES
    chip = row // CORES
    x, y = chip % SIDE, chip // SIDE
    half = col // 2
    width = parts.shape[2]
    piece = slab.shape[2]
    owners = row_count // CORES
    passes = col_count * supers

    end = (col == 0) | (col == last)

    def plan(p):
        late = p // (2 * supers)
        e = p - 2 * supers
        tail = e // (2 * (supers - 1))
        order = (1 - tail) * (2 + e // (supers - 1)) + tail * (e - 2 * (supers - 2))
        which = (1 - tail) * (e % (supers - 1)) + tail * (supers - 1)
        return (1 - late) * (p // supers) + late * order, (1 - late) * (p % supers) + late * which

    def place(o):
        far, odd = o // 2, o % 2
        return (1 - far) * (col + odd * (1 - 2 * (col % 2))) + far * ((2 - half) + odd * (1 - 2 * half))

    barrier = pltpu.get_barrier_semaphore()

    @pl.loop(1, row_count)
    def _(by):
        pl.semaphore_signal(barrier, inc=1, device_id=((row + by) % row_count, col), device_id_type=MESH)

    @pl.loop(1, col_count)
    def _(by):
        pl.semaphore_signal(barrier, inc=1, device_id=(row, (col + by) % col_count), device_id_type=MESH)

    def to(src, dst, send, recv, r, c):
        return pltpu.make_async_remote_copy(
            src_ref=src, dst_ref=dst, send_sem=send, recv_sem=recv, device_id=(r, c), device_id_type=MESH
        )

    def landed(ref, sem):
        pltpu.make_async_copy(ref, ref, sem).wait()

    def part(s, w):
        return parts.at[s, w]

    def gather(s, w, way, src):
        return to(src, part(s, w), ag_send.at[way, s, w], ag_recv.at[s, w], row, col + (1 - 2 * way))

    def chip_at(k):
        xk = (x + 1 - k % 2) % 2
        yk = (y + 1 - k // 2) % 2
        return yk * SIDE + xk

    per_pass = 2 * CHIPS

    def slab_copy(step):
        j = step % per_pass
        end, begun = j // (per_pass - 1), (j + per_pass - 1) // per_pass
        even = 1 - j % 2
        own = end + (1 - end) * even * begun
        k = (1 - end) * ((1 - even) * ((j + 1) // 2) + even * (j // 2 - begun)) + end * (CHIPS - 1)
        which = chip_at(k) * CORES + (core + 1 - own) % CORES
        off = pl.multiple_of(which * piece, piece)
        slot = step % DEPTH
        return pltpu.make_async_copy(matrix_ref.at[:, pl.ds(off, piece)], slab.at[slot], slab_sem.at[slot])

    def next_slab(step):
        slot = step % DEPTH
        landed(slab.at[slot], slab_sem.at[slot])
        return slot

    def refill(step):
        @pl.when(step + DEPTH < passes * per_pass)
        def _():
            slab_copy(step + DEPTH).start()

    def load(s):
        return pltpu.make_async_copy(factor_ref.at[s], y_ref.at[s], own_sem.at[s])

    @pl.loop(0, supers)
    def _(s):
        load(s).start()

    for step in range(DEPTH):
        slab_copy(step).start()

    def own_part(s):
        landed(y_ref.at[s], own_sem.at[s])
        parts[s, col] = (y_ref[s].astype(F32).T * mask_ref[s]).astype(BF)

    def send_own(s):
        @pl.when(col < last)
        def _():
            gather(s, col, 0, part(s, col)).start()

        @pl.when(col > 0)
        def _():
            gather(s, col, 1, part(s, col)).start()

    own_part(0)
    pl.semaphore_wait(barrier, row_count - 1 + last)

    @pl.loop(1, supers)
    def _(s):
        send_own(s - 1)
        own_part(s)

    send_own(supers - 1)

    def arrive(d, s):
        @pl.when(col >= d)
        def _():
            landed(part(s, col - d), ag_recv.at[s, col - d])

        @pl.when(col + d <= last)
        def _():
            landed(part(s, col + d), ag_recv.at[s, col + d])

    def forward(d, s):
        @pl.when((col >= d) & (col < last))
        def _():
            gather(s, col - d, 0, part(s, col - d)).start()

        @pl.when((col + d <= last) & (col > 0))
        def _():
            gather(s, col + d, 1, part(s, col + d)).start()

    def core_copy(p, k):
        return to(to_core.at[p % 2, k], from_core.at[p, k], core_send.at[p % 2, k], core_recv.at[p, k],
                  chip * CORES + 1 - core, col)

    def chip_copy(p, k):
        return to(to_chip.at[p % 2, k], from_chip.at[p, k], chip_send.at[p % 2, k], chip_recv.at[p, k],
                  chip_at(k) * CORES + core, col)

    def finish(p):
        o, s = plan(p)
        total = to_chip[p % 2, CHIPS - 1].astype(F32)
        for k in range(CHIPS - 1):
            landed(from_chip.at[p, k], chip_recv.at[p, k])
            total = total + from_chip[p, k].astype(F32)
        bank[s, o] = total.astype(BF)

    def col_copy(s, o):
        return to(bank.at[s, o], bank.at[s, col_count + col], col_send.at[s, o], col_recv.at[s, col], row, place(o))

    def row_copy(s, o, act):
        c = place(o)
        dest = CORES * c + row // owners
        q = row % owners
        src = bank.at[s, ((o + col_count - 1) // col_count) * (col_count + c)]
        remote = to(src, own_y.at[s, q], row_send.at[s, o], row_recv.at[s, q], dest, col)
        if act == "start":
            @pl.when(o > 0)
            def _():
                landed(src, col_recv.at[s, c])

            @pl.when(dest != row)
            def _():
                remote.start()

            @pl.when(dest == row)
            def _():
                pltpu.make_async_copy(src, own_y.at[s, q], row_recv.at[s, q]).start()
        else:
            @pl.when(dest != row)
            def _():
                remote.wait_send()

    def release(turn):
        for c in range(1, last):
            pl.semaphore_signal(go.at[turn], inc=1, device_id=(row, c), device_id_type=MESH)

    @pl.loop(0, passes)
    def _(p):
        o, s = plan(p)
        w = place(o)

        @pl.when((p == passes - 1) & end)
        def _():
            row_copy(0, 2, "start")
            row_copy(0, 3, "start")

        @pl.when(o > 0)
        def _():
            for d in range(1, col_count):
                @pl.when(o == d)
                def _():
                    arrive(d, s)

                    if d == 1:
                        @pl.when(s < supers - 1)
                        def _():
                            forward(1, s)
                    if d == 2:
                        forward(2, s)

                        @pl.when(s == supers - 2)
                        def _():
                            forward(1, supers - 1)

        @pl.when((p == passes - 1) & end)
        def _():
            release(0)

        @pl.when(p >= 2)
        def _():
            finish(p - 2)

        @pl.loop(0, CHIPS + 1)
        def _(k):
            @pl.when((k == 1) & (p >= 2))
            def _():
                before, which = plan(p - 2)

                @pl.when(before == 0)
                def _():
                    row_copy(which, 0, "start")

                @pl.when(((before == 1) & (end | (which < supers - 1))) | (before == 2) | ((before == 3) & (which == 0)))
                def _():
                    col_copy(which, before).start()

            @pl.when((k == 2) & (p >= passes - 1 - supers) & (p < passes - 2) & end)
            def _():
                row_copy(p - (passes - 1 - supers), 1, "start")

            @pl.when((k == 2) & (p == passes - 1) & end)
            def _():
                release(1)

            @pl.when((k == 1) & (p == passes - 1) & end)
            def _():
                @pl.loop(1, supers - 1)
                def _(e):
                    col_copy(e, 3).start()

            @pl.when(k < CHIPS)
            def _():
                @pl.when(p >= 2)
                def _():
                    core_copy(p - 2, k).wait_send()

                step = p * per_pass + 2 * k - (k + CHIPS - 1) // CHIPS
                slot = next_slab(step)

                @pl.when(k == 1)
                def _():
                    core_copy(p, 0).start()

                to_core[p % 2, k] = jnp.dot(parts[s, w], slab[slot], preferred_element_type=F32).astype(BF)
                refill(step)

                @pl.when(k >= 2)
                def _():
                    chip_copy(p, k - 2).start()

            @pl.when(k > 0)
            def _():
                step = p * per_pass + 2 * k - k // CHIPS
                slot = next_slab(step)

                @pl.when(k < CHIPS)
                def _():
                    core_copy(p, k).start()

                @pl.when(k == CHIPS)
                def _():
                    chip_copy(p, CHIPS - 2).start()

                @pl.when((p >= 2) & (k < CHIPS))
                def _():
                    chip_copy(p - 2, k - 1).wait_send()

                mine = jnp.dot(parts[s, w], slab[slot], preferred_element_type=F32)
                landed(from_core.at[p, k - 1], core_recv.at[p, k - 1])
                to_chip[p % 2, k - 1] = (mine + from_core[p, k - 1].astype(F32)).astype(BF)
                refill(step)

    def sum_copy(s, by):
        r = (row + by) % row_count
        return to(to_sum.at[s, r], from_sum.at[s, row], sum_send.at[s, r], sum_recv.at[s, row], r, col)

    def all_copy(s, by):
        r = (row + by) % row_count
        return to(all_sum.at[s, row], all_sum.at[s, row], all_send.at[s, r], all_recv.at[s, row], r, col)

    def out_copy(s):
        return pltpu.make_async_copy(y_ref.at[s], y_out.at[s], out_sem.at[0, s])

    def sum_out(s):
        return pltpu.make_async_copy(all_sum.at[s], t_out.at[s], out_sem.at[1, s])

    def settle(s):
        t_ref[...] = jnp.zeros(t_ref.shape, F32)
        for q in range(owners):
            landed(own_y.at[s, q], row_recv.at[s, q])
            here = own_y[s, q]
            off = q * piece
            mine = parts[s, :, :, pl.ds(off, piece)].reshape(t_ref.shape[0], piece)
            t_ref[...] += lax.dot_general(mine, here, (((1,), (1,)), ((), ())), preferred_element_type=F32)
        to_sum[s] = t_ref[...].reshape(to_sum.shape[1:]).astype(BF)

        def write(q):
            off = q * piece
            y_ref[s, pl.ds(off, piece), :] = (
                own_y[s, q].astype(F32) * -mask_ref[s, :, pl.ds(off, piece)]
            ).T.astype(BF)

        write(0)

        @pl.loop(1, row_count)
        def _(by):
            sum_copy(s, by).start()

        for q in range(1, owners):
            write(q)
        out_copy(s).start()

    def add_up(s):
        @pl.loop(1, row_count)
        def _(by):
            r = (row + by) % row_count
            landed(from_sum.at[s, r], sum_recv.at[s, r])

        from_sum[s, row] = to_sum[s, row]
        total = from_sum[s, 0].astype(F32)
        for r in range(1, row_count):
            total = total + from_sum[s, r].astype(F32)
        all_sum[s, row] = total.astype(BF)

        @pl.loop(1, row_count)
        def _(by):
            all_copy(s, by).start()

    def collect(s):
        @pl.loop(1, row_count)
        def _(by):
            r = (row + by) % row_count
            landed(all_sum.at[s, r], all_recv.at[s, r])

        sum_out(s).start()

    def drain_early():
        @pl.loop(0, supers)
        def _(s):
            @pl.loop(0, col_count)
            def _(w):
                @pl.when((w <= col) & (col < last))
                def _():
                    gather(s, w, 0, part(s, w)).wait_send()

                @pl.when((w >= col) & (col > 0))
                def _():
                    gather(s, w, 1, part(s, w)).wait_send()

        @pl.loop(passes - 2, passes)
        def _(p):
            @pl.loop(0, CHIPS)
            def _(k):
                core_copy(p, k).wait_send()

                @pl.when(k < CHIPS - 1)
                def _():
                    chip_copy(p, k).wait_send()

    def drain(s):
        @pl.loop(0, col_count)
        def _(o):
            row_copy(s, o, "wait")

            @pl.when(o > 0)
            def _():
                col_copy(s, o).wait_send()

        @pl.loop(1, row_count)
        def _(by):
            sum_copy(s, by).wait_send()

        out_copy(s).wait()

    finish(passes - 2)

    def middle_rows():
        @pl.loop(2, 2 * (supers - 1))
        def _(i):
            row_copy(i // 2, 2 + i % 2, "start")

    @pl.when(end)
    def _():
        col_copy(supers - 1, 2).start()
        middle_rows()

    finish(passes - 1)

    @pl.when(end)
    def _():
        col_copy(supers - 1, 3).start()

    @pl.when(jnp.logical_not(end))
    def _():
        col_copy(supers - 1, 2).start()

        @pl.loop(0, supers)
        def _(s):
            row_copy(s, 1, "start")

        row_copy(0, 2, "start")
        row_copy(0, 3, "start")
        middle_rows()

    drain_early()

    @pl.when(jnp.logical_not(end))
    def _():
        pl.semaphore_wait(go.at[0], 2)

        @pl.loop(1, supers - 1)
        def _(s):
            col_copy(s, 3).start()

        pl.semaphore_wait(go.at[1], 2)
        col_copy(supers - 1, 3).start()
        col_copy(supers - 1, 1).start()

    settle(0)
    row_copy(supers - 1, 2, "start")

    @pl.when(end)
    def _():
        row_copy(supers - 1, 1, "start")

    row_copy(supers - 1, 3, "start")

    @pl.loop(1, supers)
    def _(s):
        settle(s)

    @pl.loop(0, supers - 1)
    def _(s):
        add_up(s)

    add_up(supers - 1)

    @pl.loop(0, supers - 1)
    def _(s):
        collect(s)

    @pl.loop(0, supers)
    def _(s):
        drain(s)

    collect(supers - 1)

    @pl.loop(0, supers)
    def _(s):
        @pl.loop(1, row_count)
        def _(by):
            all_copy(s, by).wait_send()

        sum_out(s).wait()


def close(y_ref, t_ref, diag_ref, new_ref, out_ref, y, t, diag, y_sem, t_sem, diag_sem, new_sem, out_sem):
    supers = y_ref.shape[0]

    def copy(src, dst, sem):
        return pltpu.make_async_copy(src, dst, sem)

    t_in, diag_in = copy(t_ref, t, t_sem), copy(diag_ref, diag, diag_sem)
    y_in = [copy(y_ref.at[s], y.at[s], y_sem.at[s]) for s in range(supers)]
    y_over = [copy(y.at[s], new_ref.at[s], new_sem.at[s]) for s in range(supers)]
    for each in y_in + [t_in, diag_in]:
        each.start()
    for s in range(supers):
        y_in[s].wait()
        y_over[s].start()
    t_in.wait()
    diag_in.wait()
    diag[...] += t[...].astype(F32)
    over = copy(diag, out_ref, out_sem)
    over.start()
    for each in y_over + [over]:
        each.wait()


def fused(resident_inverse, factor, diag_inverse, anc_tiles, slot_tile):
    own_rows, own_cols = resident_inverse.shape
    supers, _, width = factor.shape
    row_count, col_count = lax.axis_size("row"), lax.axis_size("col")
    total_rows = own_rows * row_count
    row_mask = slot_rows(anc_tiles, slot_tile, total_rows // slot_tile.shape[0])
    own_mask = lax.dynamic_slice_in_dim(row_mask, lax.axis_index("row") * own_rows, own_rows, 1)
    piece = own_cols // row_count
    owners = row_count // CORES
    passes = col_count * supers
    wide = width * col_count
    dma = pltpu.SemaphoreType.DMA
    y, t = pl.pallas_call(
        lambda *refs: sweep(row_count, col_count, supers, *refs),
        out_shape=(
            jax.ShapeDtypeStruct((supers, own_rows, width), BF),
            jax.ShapeDtypeStruct((supers, row_count, wide // row_count, width), BF),
        ),
        in_specs=[pl.BlockSpec(memory_space=pl.ANY)] * 2 + [pl.BlockSpec(memory_space=pltpu.VMEM)],
        out_specs=[pl.BlockSpec(memory_space=pl.ANY)] * 2,
        scratch_shapes=[
            pltpu.VMEM((supers, own_rows, width), BF),
            pltpu.VMEM((wide, width), F32),
            pltpu.VMEM((DEPTH, own_rows, piece), BF),
            pltpu.VMEM((supers, col_count, width, own_rows), BF),
            pltpu.VMEM((2, CHIPS, width, piece), BF),
            pltpu.VMEM((passes, CHIPS, width, piece), BF),
            pltpu.VMEM((2, CHIPS, width, piece), BF),
            pltpu.VMEM((passes, CHIPS - 1, width, piece), BF),
            pltpu.VMEM((supers, 2 * col_count, width, piece), BF),
            pltpu.VMEM((supers, owners, width, piece), BF),
            pltpu.VMEM((supers, row_count, wide // row_count, width), BF),
            pltpu.VMEM((supers, row_count, wide // row_count, width), BF),
            pltpu.VMEM((supers, row_count, wide // row_count, width), BF),
            dma((DEPTH,)), dma((supers,)), dma((2, supers)),
            dma((2, supers, col_count)), dma((supers, col_count)),
            dma((2, CHIPS)), dma((passes, CHIPS)),
            dma((2, CHIPS)), dma((passes, CHIPS)),
            dma((supers, col_count)), dma((supers, col_count)),
            dma((supers, col_count)), dma((supers, owners)),
            dma((supers, row_count)), dma((supers, row_count)),
            dma((supers, row_count)), dma((supers, row_count)),
            pltpu.SemaphoreType.REGULAR((2,)),
        ],
        compiler_params=pltpu.CompilerParams(
            collective_id=0, has_side_effects=True, vmem_limit_bytes=67043328
        ),
    )(factor, resident_inverse, own_mask[:, None, :])
    t = t.reshape(diag_inverse.shape)
    return tuple(pl.pallas_call(
        close,
        in_specs=[pl.BlockSpec(memory_space=pl.ANY)] * 3,
        out_specs=[pl.BlockSpec(memory_space=pl.ANY)] * 2,
        out_shape=(jax.ShapeDtypeStruct(y.shape, BF), jax.ShapeDtypeStruct(t.shape, F32)),
        scratch_shapes=[
            pltpu.VMEM(y.shape, BF), pltpu.VMEM(t.shape, BF), pltpu.VMEM(t.shape, F32),
            dma((supers,)), dma(()), dma(()), dma((supers,)), dma(()),
        ],
    )(y, t, diag_inverse))


def on_device(*arrays):
    square = lax.axis_size("row") == CHIPS * CORES and lax.axis_size("col") == CHIPS
    return (fused if square else plain)(*arrays)


def solution(mesh):
    placed = (P("row", "col"), P(None, "row", "col"), P(None, None, "col"), P(), P())
    return jax.shard_map(
        on_device,
        mesh=mesh,
        in_specs=placed,
        out_specs=(P(None, "row", "col"), P(None, None, "col")),
        check_vma=False,
    )
```

```python
import jax
import jax.numpy as jnp
from jax import lax
from jax.experimental import pallas as pl
from jax.experimental.pallas import tpu as pltpu
from jax.sharding import PartitionSpec as P


def slot_rows(anc_tiles, slot_tile, tile_rows):
    listed = (anc_tiles[:, :, None] == slot_tile[None, None, :]).any(axis=1)
    return jnp.repeat(listed.astype(jnp.float32), tile_rows, axis=1)


def plain(resident_inverse, factor, diag_inverse, anc_tiles, slot_tile):
    own_rows, own_cols = resident_inverse.shape
    supers, _, part_width = factor.shape
    row_index = lax.axis_index("row")
    col_index = lax.axis_index("col")
    col_count = lax.axis_size("col")
    row_count = lax.axis_size("row")
    ratio = row_count // col_count
    owners = row_count // ratio
    total_rows = own_rows * row_count
    row_mask = slot_rows(anc_tiles, slot_tile, total_rows // slot_tile.shape[0])
    own_mask = lax.dynamic_slice_in_dim(row_mask, row_index * own_rows, own_rows, 1)
    mine = [factor[s] * own_mask[s].astype(jnp.bfloat16)[:, None] for s in range(supers)]
    last = col_count - 1
    up_moves = [(i, i + 1) for i in range(last)]
    down_moves = [(i + 1, i) for i in range(last)]
    chunk = own_cols // row_count

    parts = []
    for s in range(supers):
        ups, downs = [mine[s]], [mine[s]]
        for by in range(last):
            ups.append(lax.ppermute(ups[-1], "col", up_moves))
            downs.append(lax.ppermute(downs[-1], "col", down_moves))
        parts.append([mine[s]] + [ups[by] + downs[col_count - by] for by in range(1, col_count)])

    news, contribs = [], []
    for s in range(supers):
        wide = jnp.concatenate(parts[s], axis=1)
        partial = lax.dot_general(
            resident_inverse, wide, (((0,), (0,)), ((), ())), preferred_element_type=jnp.float32
        ).astype(jnp.bfloat16)
        summed = lax.psum_scatter(partial, "row", scatter_dimension=0, tiled=True)
        got = [summed[:, :part_width]]
        for by in range(1, col_count):
            piece = summed[:, by * part_width:(by + 1) * part_width]
            got.append(lax.ppermute(piece, "col", [(c, (c - by) % col_count) for c in range(col_count)]))
        got = jnp.stack(got)
        home = []
        for k in range(owners):
            block = (row_index + k) % owners
            piece = lax.dynamic_index_in_dim(got, (block - col_index) % col_count, 0, keepdims=False)
            moves = [(r, ratio * ((r + k) % owners) + r // owners) for r in range(row_count)]
            home.append(lax.ppermute(piece, "row", moves))
        home = jnp.stack(home)
        mine_y = jnp.concatenate([
            lax.dynamic_index_in_dim(home, (row_index // ratio - q) % owners, 0, keepdims=False)
            for q in range(owners)
        ], axis=0)
        news.append(-(mine_y * own_mask[s].astype(jnp.bfloat16)[:, None]))
        contribs.append(jnp.stack([
            jnp.einsum("rw,rv->wv", part, mine_y, preferred_element_type=jnp.float32)
            for part in parts[s]
        ]))
    stacked = jnp.stack(contribs, axis=1)
    ordered = jnp.stack([
        lax.dynamic_index_in_dim(stacked, (col_index - q) % col_count, 0, keepdims=False)
        for q in range(col_count)
    ], axis=1)
    totals = ordered.reshape(supers, col_count * part_width, part_width)
    step = 1
    while step < row_count:
        sent = totals.astype(jnp.bfloat16)
        got = lax.ppermute(sent, "row", [(i, i ^ step) for i in range(row_count)])
        totals = sent.astype(jnp.float32) + got.astype(jnp.float32)
        step *= 2
    return (jnp.stack(news), diag_inverse + totals)

MESH = pl.DeviceIdType.MESH
BF = jnp.bfloat16
F32 = jnp.float32
CORES = 2
SIDE = 2
CHIPS = SIDE * SIDE
DEPTH = 4


def sweep(row_count, col_count, supers, factor_ref, matrix_ref, mask_ref, y_out, t_out,
          y_ref, t_ref, slab, parts, to_core, from_core, to_chip, from_chip, bank, own_y, to_sum, from_sum, all_sum,
          slab_sem, own_sem, out_sem, ag_send, ag_recv, core_send, core_recv, chip_send, chip_recv,
          col_send, col_recv, row_send, row_recv, sum_send, sum_recv, all_send, all_recv, go):
    row = lax.axis_index("row")
    col = lax.axis_index("col")
    last = col_count - 1
    core = row % CORES
    chip = row // CORES
    x, y = chip % SIDE, chip // SIDE
    half = col // 2
    width = parts.shape[2]
    piece = slab.shape[2]
    owners = row_count // CORES
    passes = col_count * supers

    end = (col == 0) | (col == last)

    def plan(p):
        late = p // (2 * supers)
        e = p - 2 * supers
        tail = e // (2 * (supers - 1))
        order = (1 - tail) * (2 + e // (supers - 1)) + tail * (e - 2 * (supers - 2))
        which = (1 - tail) * (e % (supers - 1)) + tail * (supers - 1)
        return (1 - late) * (p // supers) + late * order, (1 - late) * (p % supers) + late * which

    def place(o):
        far, odd = o // 2, o % 2
        return (1 - far) * (col + odd * (1 - 2 * (col % 2))) + far * ((2 - half) + odd * (1 - 2 * half))

    barrier = pltpu.get_barrier_semaphore()

    @pl.loop(1, row_count)
    def _(by):
        pl.semaphore_signal(barrier, inc=1, device_id=((row + by) % row_count, col), device_id_type=MESH)

    @pl.loop(1, col_count)
    def _(by):
        pl.semaphore_signal(barrier, inc=1, device_id=(row, (col + by) % col_count), device_id_type=MESH)

    def to(src, dst, send, recv, r, c):
        return pltpu.make_async_remote_copy(
            src_ref=src, dst_ref=dst, send_sem=send, recv_sem=recv, device_id=(r, c), device_id_type=MESH
        )

    def landed(ref, sem):
        pltpu.make_async_copy(ref, ref, sem).wait()

    def part(s, w):
        return parts.at[s, w]

    def gather(s, w, way, src):
        return to(src, part(s, w), ag_send.at[way, s, w], ag_recv.at[s, w], row, col + (1 - 2 * way))

    def chip_at(k):
        xk = (x + 1 - k % 2) % 2
        yk = (y + 1 - k // 2) % 2
        return yk * SIDE + xk

    per_pass = 2 * CHIPS

    def slab_copy(step):
        j = step % per_pass
        end, begun = j // (per_pass - 1), (j + per_pass - 1) // per_pass
        even = 1 - j % 2
        own = end + (1 - end) * even * begun
        k = (1 - end) * ((1 - even) * ((j + 1) // 2) + even * (j // 2 - begun)) + end * (CHIPS - 1)
        which = chip_at(k) * CORES + (core + 1 - own) % CORES
        off = pl.multiple_of(which * piece, piece)
        slot = step % DEPTH
        return pltpu.make_async_copy(matrix_ref.at[:, pl.ds(off, piece)], slab.at[slot], slab_sem.at[slot])

    def next_slab(step):
        slot = step % DEPTH
        landed(slab.at[slot], slab_sem.at[slot])
        return slot

    def refill(step):
        @pl.when(step + DEPTH < passes * per_pass)
        def _():
            slab_copy(step + DEPTH).start()

    def load(s):
        return pltpu.make_async_copy(factor_ref.at[s], y_ref.at[s], own_sem.at[s])

    @pl.loop(0, supers)
    def _(s):
        load(s).start()

    for step in range(DEPTH):
        slab_copy(step).start()

    def own_part(s):
        landed(y_ref.at[s], own_sem.at[s])
        parts[s, col] = (y_ref[s].astype(F32).T * mask_ref[s]).astype(BF)

    def send_own(s):
        @pl.when(col < last)
        def _():
            gather(s, col, 0, part(s, col)).start()

        @pl.when(col > 0)
        def _():
            gather(s, col, 1, part(s, col)).start()

    own_part(0)
    pl.semaphore_wait(barrier, row_count - 1 + last)

    @pl.loop(1, supers)
    def _(s):
        send_own(s - 1)
        own_part(s)

    send_own(supers - 1)

    def arrive(d, s):
        @pl.when(col >= d)
        def _():
            landed(part(s, col - d), ag_recv.at[s, col - d])

        @pl.when(col + d <= last)
        def _():
            landed(part(s, col + d), ag_recv.at[s, col + d])

    def forward(d, s):
        @pl.when((col >= d) & (col < last))
        def _():
            gather(s, col - d, 0, part(s, col - d)).start()

        @pl.when((col + d <= last) & (col > 0))
        def _():
            gather(s, col + d, 1, part(s, col + d)).start()

    def core_copy(p, k):
        return to(to_core.at[p % 2, k], from_core.at[p, k], core_send.at[p % 2, k], core_recv.at[p, k],
                  chip * CORES + 1 - core, col)

    def chip_copy(p, k):
        return to(to_chip.at[p % 2, k], from_chip.at[p, k], chip_send.at[p % 2, k], chip_recv.at[p, k],
                  chip_at(k) * CORES + core, col)

    def finish(p):
        o, s = plan(p)
        total = to_chip[p % 2, CHIPS - 1].astype(F32)
        for k in range(CHIPS - 1):
            landed(from_chip.at[p, k], chip_recv.at[p, k])
            total = total + from_chip[p, k].astype(F32)
        bank[s, o] = total.astype(BF)

    def col_copy(s, o):
        return to(bank.at[s, o], bank.at[s, col_count + col], col_send.at[s, o], col_recv.at[s, col], row, place(o))

    def row_copy(s, o, act):
        c = place(o)
        dest = CORES * c + row // owners
        q = row % owners
        src = bank.at[s, ((o + col_count - 1) // col_count) * (col_count + c)]
        remote = to(src, own_y.at[s, q], row_send.at[s, o], row_recv.at[s, q], dest, col)
        if act == "start":
            @pl.when(o > 0)
            def _():
                landed(src, col_recv.at[s, c])

            @pl.when(dest != row)
            def _():
                remote.start()

            @pl.when(dest == row)
            def _():
                pltpu.make_async_copy(src, own_y.at[s, q], row_recv.at[s, q]).start()
        else:
            @pl.when(dest != row)
            def _():
                remote.wait_send()

    def release(turn):
        for c in range(1, last):
            pl.semaphore_signal(go.at[turn], inc=1, device_id=(row, c), device_id_type=MESH)

    @pl.loop(0, passes)
    def _(p):
        o, s = plan(p)
        w = place(o)

        @pl.when((p == passes - 1) & end)
        def _():
            row_copy(0, 2, "start")
            row_copy(0, 3, "start")

        @pl.when(o > 0)
        def _():
            for d in range(1, col_count):
                @pl.when(o == d)
                def _():
                    arrive(d, s)

                    if d == 1:
                        @pl.when(s < supers - 1)
                        def _():
                            forward(1, s)
                    if d == 2:
                        forward(2, s)

                        @pl.when(s == supers - 2)
                        def _():
                            forward(1, supers - 1)

        @pl.when((p == passes - 1) & end)
        def _():
            release(0)

        @pl.when(p >= 2)
        def _():
            finish(p - 2)

        @pl.loop(0, CHIPS + 1)
        def _(k):
            @pl.when((k == 1) & (p >= 2))
            def _():
                before, which = plan(p - 2)

                @pl.when(before == 0)
                def _():
                    row_copy(which, 0, "start")

                @pl.when(((before == 1) & (end | (which < supers - 1))) | (before == 2) | ((before == 3) & (which == 0)))
                def _():
                    col_copy(which, before).start()

            @pl.when((k == 2) & (p >= passes - 1 - supers) & (p < passes - 2) & end)
            def _():
                row_copy(p - (passes - 1 - supers), 1, "start")

            @pl.when((k == 2) & (p == passes - 1) & end)
            def _():
                release(1)

            @pl.when((k == 1) & (p == passes - 1) & end)
            def _():
                @pl.loop(1, supers - 1)
                def _(e):
                    col_copy(e, 3).start()

            @pl.when(k < CHIPS)
            def _():
                @pl.when(p >= 2)
                def _():
                    core_copy(p - 2, k).wait_send()

                step = p * per_pass + 2 * k - (k + CHIPS - 1) // CHIPS
                slot = next_slab(step)

                @pl.when(k == 1)
                def _():
                    core_copy(p, 0).start()

                to_core[p % 2, k] = jnp.dot(parts[s, w], slab[slot], preferred_element_type=F32).astype(BF)
                refill(step)

                @pl.when(k >= 2)
                def _():
                    chip_copy(p, k - 2).start()

            @pl.when(k > 0)
            def _():
                step = p * per_pass + 2 * k - k // CHIPS
                slot = next_slab(step)

                @pl.when(k < CHIPS)
                def _():
                    core_copy(p, k).start()

                @pl.when(k == CHIPS)
                def _():
                    chip_copy(p, CHIPS - 2).start()

                @pl.when((p >= 2) & (k < CHIPS))
                def _():
                    chip_copy(p - 2, k - 1).wait_send()

                mine = jnp.dot(parts[s, w], slab[slot], preferred_element_type=F32)
                landed(from_core.at[p, k - 1], core_recv.at[p, k - 1])
                to_chip[p % 2, k - 1] = (mine + from_core[p, k - 1].astype(F32)).astype(BF)
                refill(step)

    def sum_copy(s, by):
        r = (row + by) % row_count
        return to(to_sum.at[s, r], from_sum.at[s, row], sum_send.at[s, r], sum_recv.at[s, row], r, col)

    def all_copy(s, by):
        r = (row + by) % row_count
        return to(all_sum.at[s], t_out.at[s, row], all_send.at[s, r], all_recv.at[s, row], r, col)

    def out_copy(s):
        return pltpu.make_async_copy(y_ref.at[s], y_out.at[s], out_sem.at[0, s])

    def sum_out(s):
        return pltpu.make_async_copy(all_sum.at[s], t_out.at[s, row], out_sem.at[1, s])

    def settle(s):
        t_ref[...] = jnp.zeros(t_ref.shape, F32)
        for q in range(owners):
            landed(own_y.at[s, q], row_recv.at[s, q])
            here = own_y[s, q]
            off = q * piece
            mine = parts[s, :, :, pl.ds(off, piece)].reshape(t_ref.shape[0], piece)
            t_ref[...] += lax.dot_general(mine, here, (((1,), (1,)), ((), ())), preferred_element_type=F32)
        to_sum[s] = t_ref[...].reshape(to_sum.shape[1:]).astype(BF)

        def write(q):
            off = q * piece
            y_ref[s, pl.ds(off, piece), :] = (
                own_y[s, q].astype(F32) * -mask_ref[s, :, pl.ds(off, piece)]
            ).T.astype(BF)

        write(0)

        @pl.loop(1, row_count)
        def _(by):
            sum_copy(s, by).start()

        for q in range(1, owners):
            write(q)
        out_copy(s).start()

    def add_up(s):
        @pl.loop(1, row_count)
        def _(by):
            r = (row + by) % row_count
            landed(from_sum.at[s, r], sum_recv.at[s, r])

        from_sum[s, row] = to_sum[s, row]
        total = from_sum[s, 0].astype(F32)
        for r in range(1, row_count):
            total = total + from_sum[s, r].astype(F32)
        all_sum[s] = total.astype(BF)

        @pl.loop(1, row_count)
        def _(by):
            all_copy(s, by).start()

        sum_out(s).start()

    def collect(s):
        @pl.loop(1, row_count)
        def _(by):
            r = (row + by) % row_count
            landed(t_out.at[s, r], all_recv.at[s, r])

    def drain_early():
        @pl.loop(0, supers)
        def _(s):
            @pl.loop(0, col_count)
            def _(w):
                @pl.when((w <= col) & (col < last))
                def _():
                    gather(s, w, 0, part(s, w)).wait_send()

                @pl.when((w >= col) & (col > 0))
                def _():
                    gather(s, w, 1, part(s, w)).wait_send()

        @pl.loop(passes - 2, passes)
        def _(p):
            @pl.loop(0, CHIPS)
            def _(k):
                core_copy(p, k).wait_send()

                @pl.when(k < CHIPS - 1)
                def _():
                    chip_copy(p, k).wait_send()

    def drain(s):
        @pl.loop(0, col_count)
        def _(o):
            row_copy(s, o, "wait")

            @pl.when(o > 0)
            def _():
                col_copy(s, o).wait_send()

        @pl.loop(1, row_count)
        def _(by):
            sum_copy(s, by).wait_send()

        out_copy(s).wait()

    finish(passes - 2)

    def middle_rows():
        @pl.loop(2, 2 * (supers - 1))
        def _(i):
            row_copy(i // 2, 2 + i % 2, "start")

    @pl.when(end)
    def _():
        col_copy(supers - 1, 2).start()
        middle_rows()

    finish(passes - 1)

    @pl.when(end)
    def _():
        col_copy(supers - 1, 3).start()

    @pl.when(jnp.logical_not(end))
    def _():
        col_copy(supers - 1, 2).start()

        @pl.loop(0, supers)
        def _(s):
            row_copy(s, 1, "start")

        row_copy(0, 2, "start")
        row_copy(0, 3, "start")
        middle_rows()

    drain_early()

    @pl.when(jnp.logical_not(end))
    def _():
        pl.semaphore_wait(go.at[0], 2)

        @pl.loop(1, supers - 1)
        def _(s):
            col_copy(s, 3).start()

        pl.semaphore_wait(go.at[1], 2)
        col_copy(supers - 1, 3).start()
        col_copy(supers - 1, 1).start()

    settle(0)
    row_copy(supers - 1, 2, "start")

    @pl.when(end)
    def _():
        row_copy(supers - 1, 1, "start")

    row_copy(supers - 1, 3, "start")

    settle(1)
    add_up(0)

    @pl.loop(2, supers)
    def _(s):
        settle(s)

    @pl.loop(1, supers - 1)
    def _(s):
        add_up(s)

    add_up(supers - 1)

    @pl.loop(0, supers - 1)
    def _(s):
        collect(s)

    @pl.loop(0, supers)
    def _(s):
        drain(s)

    collect(supers - 1)

    @pl.loop(0, supers)
    def _(s):
        @pl.loop(1, row_count)
        def _(by):
            all_copy(s, by).wait_send()

        sum_out(s).wait()


def close(y_ref, t_ref, diag_ref, new_ref, out_ref, y, t, diag, y_sem, t_sem, diag_sem, new_sem, out_sem):
    supers = y_ref.shape[0]

    def copy(src, dst, sem):
        return pltpu.make_async_copy(src, dst, sem)

    t_in, diag_in = copy(t_ref, t, t_sem), copy(diag_ref, diag, diag_sem)
    half = y_ref.shape[1] // 2
    parts = [(s, pl.ds(h * half, half)) for s in range(supers) for h in range(2)]
    y_in = [copy(y_ref.at[at], y.at[at], y_sem.at[i]) for i, at in enumerate(parts)]
    y_over = [copy(y.at[at], new_ref.at[at], new_sem.at[i]) for i, at in enumerate(parts)]
    for each in y_in + [t_in, diag_in]:
        each.start()
    for came, goes in zip(y_in, y_over):
        came.wait()
        goes.start()
    t_in.wait()
    diag_in.wait()
    diag[...] += t[...].astype(F32)
    over = copy(diag, out_ref, out_sem)
    over.start()
    for each in y_over + [over]:
        each.wait()


def fused(resident_inverse, factor, diag_inverse, anc_tiles, slot_tile):
    own_rows, own_cols = resident_inverse.shape
    supers, _, width = factor.shape
    row_count, col_count = lax.axis_size("row"), lax.axis_size("col")
    total_rows = own_rows * row_count
    row_mask = slot_rows(anc_tiles, slot_tile, total_rows // slot_tile.shape[0])
    own_mask = lax.dynamic_slice_in_dim(row_mask, lax.axis_index("row") * own_rows, own_rows, 1)
    piece = own_cols // row_count
    owners = row_count // CORES
    passes = col_count * supers
    wide = width * col_count
    dma = pltpu.SemaphoreType.DMA
    y, t = pl.pallas_call(
        lambda *refs: sweep(row_count, col_count, supers, *refs),
        out_shape=(
            jax.ShapeDtypeStruct((supers, own_rows, width), BF),
            jax.ShapeDtypeStruct((supers, row_count, wide // row_count, width), BF),
        ),
        in_specs=[pl.BlockSpec(memory_space=pl.ANY)] * 2 + [pl.BlockSpec(memory_space=pltpu.VMEM)],
        out_specs=[pl.BlockSpec(memory_space=pl.ANY)] * 2,
        scratch_shapes=[
            pltpu.VMEM((supers, own_rows, width), BF),
            pltpu.VMEM((wide, width), F32),
            pltpu.VMEM((DEPTH, own_rows, piece), BF),
            pltpu.VMEM((supers, col_count, width, own_rows), BF),
            pltpu.VMEM((2, CHIPS, width, piece), BF),
            pltpu.VMEM((passes, CHIPS, width, piece), BF),
            pltpu.VMEM((2, CHIPS, width, piece), BF),
            pltpu.VMEM((passes, CHIPS - 1, width, piece), BF),
            pltpu.VMEM((supers, 2 * col_count, width, piece), BF),
            pltpu.VMEM((supers, owners, width, piece), BF),
            pltpu.VMEM((supers, row_count, wide // row_count, width), BF),
            pltpu.VMEM((supers, row_count, wide // row_count, width), BF),
            pltpu.VMEM((supers, wide // row_count, width), BF),
            dma((DEPTH,)), dma((supers,)), dma((2, supers)),
            dma((2, supers, col_count)), dma((supers, col_count)),
            dma((2, CHIPS)), dma((passes, CHIPS)),
            dma((2, CHIPS)), dma((passes, CHIPS)),
            dma((supers, col_count)), dma((supers, col_count)),
            dma((supers, col_count)), dma((supers, owners)),
            dma((supers, row_count)), dma((supers, row_count)),
            dma((supers, row_count)), dma((supers, row_count)),
            pltpu.SemaphoreType.REGULAR((2,)),
        ],
        compiler_params=pltpu.CompilerParams(
            collective_id=0, has_side_effects=True, vmem_limit_bytes=67043328
        ),
    )(factor, resident_inverse, own_mask[:, None, :])
    t = t.reshape(diag_inverse.shape)
    return tuple(pl.pallas_call(
        close,
        in_specs=[pl.BlockSpec(memory_space=pl.ANY)] * 3,
        out_specs=[pl.BlockSpec(memory_space=pl.ANY)] * 2,
        out_shape=(jax.ShapeDtypeStruct(y.shape, BF), jax.ShapeDtypeStruct(t.shape, F32)),
        scratch_shapes=[
            pltpu.VMEM(y.shape, BF), pltpu.VMEM(t.shape, BF), pltpu.VMEM(t.shape, F32),
            dma((2 * supers,)), dma(()), dma(()), dma((2 * supers,)), dma(()),
        ],
    )(y, t, diag_inverse))


def on_device(*arrays):
    square = lax.axis_size("row") == CHIPS * CORES and lax.axis_size("col") == CHIPS
    return (fused if square else plain)(*arrays)


def solution(mesh):
    placed = (P("row", "col"), P(None, "row", "col"), P(None, None, "col"), P(), P())
    return jax.shard_map(
        on_device,
        mesh=mesh,
        in_specs=placed,
        out_specs=(P(None, "row", "col"), P(None, None, "col")),
        check_vma=False,
    )
```

```python
import jax
import jax.numpy as jnp
from jax import lax
from jax.experimental import pallas as pl
from jax.experimental.pallas import tpu as pltpu
from jax.sharding import PartitionSpec as P


def slot_rows(anc_tiles, slot_tile, tile_rows):
    listed = (anc_tiles[:, :, None] == slot_tile[None, None, :]).any(axis=1)
    return jnp.repeat(listed.astype(jnp.float32), tile_rows, axis=1)


def plain(resident_inverse, factor, diag_inverse, anc_tiles, slot_tile):
    own_rows, own_cols = resident_inverse.shape
    supers, _, part_width = factor.shape
    row_index = lax.axis_index("row")
    col_index = lax.axis_index("col")
    col_count = lax.axis_size("col")
    row_count = lax.axis_size("row")
    ratio = row_count // col_count
    owners = row_count // ratio
    total_rows = own_rows * row_count
    row_mask = slot_rows(anc_tiles, slot_tile, total_rows // slot_tile.shape[0])
    own_mask = lax.dynamic_slice_in_dim(row_mask, row_index * own_rows, own_rows, 1)
    mine = [factor[s] * own_mask[s].astype(jnp.bfloat16)[:, None] for s in range(supers)]
    last = col_count - 1
    up_moves = [(i, i + 1) for i in range(last)]
    down_moves = [(i + 1, i) for i in range(last)]
    chunk = own_cols // row_count

    parts = []
    for s in range(supers):
        ups, downs = [mine[s]], [mine[s]]
        for by in range(last):
            ups.append(lax.ppermute(ups[-1], "col", up_moves))
            downs.append(lax.ppermute(downs[-1], "col", down_moves))
        parts.append([mine[s]] + [ups[by] + downs[col_count - by] for by in range(1, col_count)])

    news, contribs = [], []
    for s in range(supers):
        wide = jnp.concatenate(parts[s], axis=1)
        partial = lax.dot_general(
            resident_inverse, wide, (((0,), (0,)), ((), ())), preferred_element_type=jnp.float32
        ).astype(jnp.bfloat16)
        summed = lax.psum_scatter(partial, "row", scatter_dimension=0, tiled=True)
        got = [summed[:, :part_width]]
        for by in range(1, col_count):
            piece = summed[:, by * part_width:(by + 1) * part_width]
            got.append(lax.ppermute(piece, "col", [(c, (c - by) % col_count) for c in range(col_count)]))
        got = jnp.stack(got)
        home = []
        for k in range(owners):
            block = (row_index + k) % owners
            piece = lax.dynamic_index_in_dim(got, (block - col_index) % col_count, 0, keepdims=False)
            moves = [(r, ratio * ((r + k) % owners) + r // owners) for r in range(row_count)]
            home.append(lax.ppermute(piece, "row", moves))
        home = jnp.stack(home)
        mine_y = jnp.concatenate([
            lax.dynamic_index_in_dim(home, (row_index // ratio - q) % owners, 0, keepdims=False)
            for q in range(owners)
        ], axis=0)
        news.append(-(mine_y * own_mask[s].astype(jnp.bfloat16)[:, None]))
        contribs.append(jnp.stack([
            jnp.einsum("rw,rv->wv", part, mine_y, preferred_element_type=jnp.float32)
            for part in parts[s]
        ]))
    stacked = jnp.stack(contribs, axis=1)
    ordered = jnp.stack([
        lax.dynamic_index_in_dim(stacked, (col_index - q) % col_count, 0, keepdims=False)
        for q in range(col_count)
    ], axis=1)
    totals = ordered.reshape(supers, col_count * part_width, part_width)
    step = 1
    while step < row_count:
        sent = totals.astype(jnp.bfloat16)
        got = lax.ppermute(sent, "row", [(i, i ^ step) for i in range(row_count)])
        totals = sent.astype(jnp.float32) + got.astype(jnp.float32)
        step *= 2
    return (jnp.stack(news), diag_inverse + totals)

MESH = pl.DeviceIdType.MESH
BF = jnp.bfloat16
F32 = jnp.float32
CORES = 2
SIDE = 2
CHIPS = SIDE * SIDE
DEPTH = 4
STRIPS = 2


def sweep(row_count, col_count, supers, factor_ref, matrix_ref, mask_ref, y_out, t_out,
          y_ref, t_ref, slab, parts, to_core, from_core, to_chip, from_chip, bank, own_y, to_sum, from_sum, all_sum,
          slab_sem, own_sem, out_sem, ag_send, ag_recv, core_send, core_recv, chip_send, chip_recv,
          col_send, col_recv, row_send, row_recv, sum_send, sum_recv, all_send, all_recv, go):
    row = lax.axis_index("row")
    col = lax.axis_index("col")
    last = col_count - 1
    core = row % CORES
    chip = row // CORES
    x, y = chip % SIDE, chip // SIDE
    half = col // 2
    width = parts.shape[2]
    piece = slab.shape[2]
    owners = row_count // CORES
    passes = col_count * supers

    end = (col == 0) | (col == last)

    def plan(p):
        late = p // (2 * supers)
        e = p - 2 * supers
        tail = e // (2 * (supers - 1))
        order = (1 - tail) * (2 + e // (supers - 1)) + tail * (e - 2 * (supers - 2))
        which = (1 - tail) * (e % (supers - 1)) + tail * (supers - 1)
        return (1 - late) * (p // supers) + late * order, (1 - late) * (p % supers) + late * which

    def place(o):
        far, odd = o // 2, o % 2
        return (1 - far) * (col + odd * (1 - 2 * (col % 2))) + far * ((2 - half) + odd * (1 - 2 * half))

    barrier = pltpu.get_barrier_semaphore()

    @pl.loop(1, row_count)
    def _(by):
        pl.semaphore_signal(barrier, inc=1, device_id=((row + by) % row_count, col), device_id_type=MESH)

    @pl.loop(1, col_count)
    def _(by):
        pl.semaphore_signal(barrier, inc=1, device_id=(row, (col + by) % col_count), device_id_type=MESH)

    def to(src, dst, send, recv, r, c):
        return pltpu.make_async_remote_copy(
            src_ref=src, dst_ref=dst, send_sem=send, recv_sem=recv, device_id=(r, c), device_id_type=MESH
        )

    def landed(ref, sem):
        pltpu.make_async_copy(ref, ref, sem).wait()

    def part(s, w):
        return parts.at[s, w]

    def gather(s, w, way, src):
        return to(src, part(s, w), ag_send.at[way, s, w], ag_recv.at[s, w], row, col + (1 - 2 * way))

    def chip_at(k):
        xk = (x + 1 - k % 2) % 2
        yk = (y + 1 - k // 2) % 2
        return yk * SIDE + xk

    per_pass = 2 * CHIPS

    def slab_copy(step):
        j = step % per_pass
        end, begun = j // (per_pass - 1), (j + per_pass - 1) // per_pass
        even = 1 - j % 2
        own = end + (1 - end) * even * begun
        k = (1 - end) * ((1 - even) * ((j + 1) // 2) + even * (j // 2 - begun)) + end * (CHIPS - 1)
        which = chip_at(k) * CORES + (core + 1 - own) % CORES
        off = pl.multiple_of(which * piece, piece)
        slot = step % DEPTH
        return pltpu.make_async_copy(matrix_ref.at[:, pl.ds(off, piece)], slab.at[slot], slab_sem.at[slot])

    def next_slab(step):
        slot = step % DEPTH
        landed(slab.at[slot], slab_sem.at[slot])
        return slot

    def refill(step):
        @pl.when(step + DEPTH < passes * per_pass)
        def _():
            slab_copy(step + DEPTH).start()

    def load(s):
        return pltpu.make_async_copy(factor_ref.at[s], y_ref.at[s], own_sem.at[s])

    @pl.loop(0, supers)
    def _(s):
        load(s).start()

    for step in range(DEPTH):
        slab_copy(step).start()

    def own_part(s):
        landed(y_ref.at[s], own_sem.at[s])
        parts[s, col] = (y_ref[s].astype(F32).T * mask_ref[s]).astype(BF)

    def send_own(s):
        @pl.when(col < last)
        def _():
            gather(s, col, 0, part(s, col)).start()

        @pl.when(col > 0)
        def _():
            gather(s, col, 1, part(s, col)).start()

    own_part(0)
    pl.semaphore_wait(barrier, row_count - 1 + last)

    @pl.loop(1, supers)
    def _(s):
        send_own(s - 1)
        own_part(s)

    send_own(supers - 1)

    def arrive(d, s):
        @pl.when(col >= d)
        def _():
            landed(part(s, col - d), ag_recv.at[s, col - d])

        @pl.when(col + d <= last)
        def _():
            landed(part(s, col + d), ag_recv.at[s, col + d])

    def forward(d, s):
        @pl.when((col >= d) & (col < last))
        def _():
            gather(s, col - d, 0, part(s, col - d)).start()

        @pl.when((col + d <= last) & (col > 0))
        def _():
            gather(s, col + d, 1, part(s, col + d)).start()

    def core_copy(p, k):
        return to(to_core.at[p % 2, k], from_core.at[p, k], core_send.at[p % 2, k], core_recv.at[p, k],
                  chip * CORES + 1 - core, col)

    def chip_copy(p, k):
        return to(to_chip.at[p % 2, k], from_chip.at[p, k], chip_send.at[p % 2, k], chip_recv.at[p, k],
                  chip_at(k) * CORES + core, col)

    def finish(p):
        o, s = plan(p)
        total = to_chip[p % 2, CHIPS - 1].astype(F32)
        for k in range(CHIPS - 1):
            landed(from_chip.at[p, k], chip_recv.at[p, k])
            total = total + from_chip[p, k].astype(F32)
        bank[s, o] = total.astype(BF)

    def strip(h):
        return pl.ds(h * (width // STRIPS), width // STRIPS)

    def col_copy(s, o, h):
        return to(bank.at[s, o, strip(h)], bank.at[s, col_count + col, strip(h)],
                  col_send.at[s, o, h], col_recv.at[s, col, h], row, place(o))

    def col_start(s, o):
        for h in range(STRIPS):
            col_copy(s, o, h).start()

    def row_copy(s, o, act):
        c = place(o)
        dest = CORES * c + row // owners
        q = row % owners
        at = ((o + col_count - 1) // col_count) * (col_count + c)
        for h in range(STRIPS):
            src, dst = bank.at[s, at, strip(h)], own_y.at[s, q, strip(h)]
            remote = to(src, dst, row_send.at[s, o, h], row_recv.at[s, q, h], dest, col)
            if act == "start":
                @pl.when(o > 0)
                def _():
                    landed(src, col_recv.at[s, c, h])

                @pl.when(dest != row)
                def _():
                    remote.start()

                @pl.when(dest == row)
                def _():
                    pltpu.make_async_copy(src, dst, row_recv.at[s, q, h]).start()
            else:
                @pl.when(dest != row)
                def _():
                    remote.wait_send()

    def release(turn):
        for c in range(1, last):
            pl.semaphore_signal(go.at[turn], inc=1, device_id=(row, c), device_id_type=MESH)

    @pl.loop(0, passes)
    def _(p):
        o, s = plan(p)
        w = place(o)

        @pl.when((p == passes - 1) & end)
        def _():
            row_copy(0, 2, "start")
            row_copy(0, 3, "start")

        @pl.when(o > 0)
        def _():
            for d in range(1, col_count):
                @pl.when(o == d)
                def _():
                    arrive(d, s)

                    if d == 1:
                        @pl.when(s < supers - 1)
                        def _():
                            forward(1, s)
                    if d == 2:
                        forward(2, s)

                        @pl.when(s == supers - 2)
                        def _():
                            forward(1, supers - 1)

        @pl.when((p == passes - 1) & end)
        def _():
            release(0)

        @pl.when(p >= 2)
        def _():
            finish(p - 2)

        @pl.loop(0, CHIPS + 1)
        def _(k):
            @pl.when((k == 1) & (p >= 2))
            def _():
                before, which = plan(p - 2)

                @pl.when(before == 0)
                def _():
                    row_copy(which, 0, "start")

                @pl.when(((before == 1) & (end | (which < supers - 1))) | (before == 2) | ((before == 3) & (which == 0)))
                def _():
                    col_start(which, before)

            @pl.when((k == 2) & (p >= passes - 1 - supers) & (p < passes - 2) & end)
            def _():
                row_copy(p - (passes - 1 - supers), 1, "start")

            @pl.when((k == 2) & (p == passes - 1) & end)
            def _():
                release(1)

            @pl.when((k == 1) & (p == passes - 1) & end)
            def _():
                @pl.loop(1, supers - 1)
                def _(e):
                    col_start(e, 3)

            @pl.when(k < CHIPS)
            def _():
                @pl.when(p >= 2)
                def _():
                    core_copy(p - 2, k).wait_send()

                step = p * per_pass + 2 * k - (k + CHIPS - 1) // CHIPS
                slot = next_slab(step)

                @pl.when(k == 1)
                def _():
                    core_copy(p, 0).start()

                to_core[p % 2, k] = jnp.dot(parts[s, w], slab[slot], preferred_element_type=F32).astype(BF)
                refill(step)

                @pl.when(k >= 2)
                def _():
                    chip_copy(p, k - 2).start()

            @pl.when(k > 0)
            def _():
                step = p * per_pass + 2 * k - k // CHIPS
                slot = next_slab(step)

                @pl.when(k < CHIPS)
                def _():
                    core_copy(p, k).start()

                @pl.when(k == CHIPS)
                def _():
                    chip_copy(p, CHIPS - 2).start()

                @pl.when((p >= 2) & (k < CHIPS))
                def _():
                    chip_copy(p - 2, k - 1).wait_send()

                mine = jnp.dot(parts[s, w], slab[slot], preferred_element_type=F32)
                landed(from_core.at[p, k - 1], core_recv.at[p, k - 1])
                to_chip[p % 2, k - 1] = (mine + from_core[p, k - 1].astype(F32)).astype(BF)
                refill(step)

    def sum_copy(s, by):
        r = (row + by) % row_count
        return to(to_sum.at[s, r], from_sum.at[s, row], sum_send.at[s, r], sum_recv.at[s, row], r, col)

    def all_copy(s, by):
        r = (row + by) % row_count
        return to(all_sum.at[s], t_out.at[s, row], all_send.at[s, r], all_recv.at[s, row], r, col)

    def out_copy(s):
        return pltpu.make_async_copy(y_ref.at[s], y_out.at[s], out_sem.at[0, s])

    def sum_out(s):
        return pltpu.make_async_copy(all_sum.at[s], t_out.at[s, row], out_sem.at[1, s])

    def settle(s):
        t_ref[...] = jnp.zeros(t_ref.shape, F32)
        for q in range(owners):
            for h in range(STRIPS):
                landed(own_y.at[s, q, strip(h)], row_recv.at[s, q, h])
            here = own_y[s, q]
            off = q * piece
            mine = parts[s, :, :, pl.ds(off, piece)].reshape(t_ref.shape[0], piece)
            t_ref[...] += lax.dot_general(mine, here, (((1,), (1,)), ((), ())), preferred_element_type=F32)
        to_sum[s] = t_ref[...].reshape(to_sum.shape[1:]).astype(BF)

        def write(q):
            off = q * piece
            y_ref[s, pl.ds(off, piece), :] = (
                own_y[s, q].astype(F32) * -mask_ref[s, :, pl.ds(off, piece)]
            ).T.astype(BF)

        write(0)

        @pl.loop(1, row_count)
        def _(by):
            sum_copy(s, by).start()

        for q in range(1, owners):
            write(q)
        out_copy(s).start()

    def add_up(s):
        @pl.loop(1, row_count)
        def _(by):
            r = (row + by) % row_count
            landed(from_sum.at[s, r], sum_recv.at[s, r])

        from_sum[s, row] = to_sum[s, row]
        total = from_sum[s, 0].astype(F32)
        for r in range(1, row_count):
            total = total + from_sum[s, r].astype(F32)
        all_sum[s] = total.astype(BF)

        @pl.loop(1, row_count)
        def _(by):
            all_copy(s, by).start()

        sum_out(s).start()

    def collect(s):
        @pl.loop(1, row_count)
        def _(by):
            r = (row + by) % row_count
            landed(t_out.at[s, r], all_recv.at[s, r])

    def drain_early():
        @pl.loop(0, supers)
        def _(s):
            @pl.loop(0, col_count)
            def _(w):
                @pl.when((w <= col) & (col < last))
                def _():
                    gather(s, w, 0, part(s, w)).wait_send()

                @pl.when((w >= col) & (col > 0))
                def _():
                    gather(s, w, 1, part(s, w)).wait_send()

        @pl.loop(passes - 2, passes)
        def _(p):
            @pl.loop(0, CHIPS)
            def _(k):
                core_copy(p, k).wait_send()

                @pl.when(k < CHIPS - 1)
                def _():
                    chip_copy(p, k).wait_send()

    def drain(s):
        @pl.loop(0, col_count)
        def _(o):
            row_copy(s, o, "wait")

            @pl.when(o > 0)
            def _():
                for h in range(STRIPS):
                    col_copy(s, o, h).wait_send()

        @pl.loop(1, row_count)
        def _(by):
            sum_copy(s, by).wait_send()

        out_copy(s).wait()

    finish(passes - 2)

    def middle_rows():
        @pl.loop(2, 2 * (supers - 1))
        def _(i):
            row_copy(i // 2, 2 + i % 2, "start")

    @pl.when(end)
    def _():
        col_start(supers - 1, 2)
        middle_rows()

    finish(passes - 1)

    @pl.when(end)
    def _():
        col_start(supers - 1, 3)

    @pl.when(jnp.logical_not(end))
    def _():
        col_start(supers - 1, 2)

        @pl.loop(0, supers)
        def _(s):
            row_copy(s, 1, "start")

        row_copy(0, 2, "start")
        row_copy(0, 3, "start")
        middle_rows()

    drain_early()

    @pl.when(jnp.logical_not(end))
    def _():
        pl.semaphore_wait(go.at[0], 2)

        @pl.loop(1, supers - 1)
        def _(s):
            col_start(s, 3)

        pl.semaphore_wait(go.at[1], 2)
        col_start(supers - 1, 3)
        col_start(supers - 1, 1)

    settle(0)
    row_copy(supers - 1, 2, "start")

    @pl.when(end)
    def _():
        row_copy(supers - 1, 1, "start")

    row_copy(supers - 1, 3, "start")

    settle(1)
    add_up(0)

    @pl.loop(2, supers)
    def _(s):
        settle(s)

    @pl.loop(1, supers - 1)
    def _(s):
        add_up(s)

    add_up(supers - 1)

    @pl.loop(0, supers - 1)
    def _(s):
        collect(s)

    @pl.loop(0, supers)
    def _(s):
        drain(s)

    collect(supers - 1)

    @pl.loop(0, supers)
    def _(s):
        @pl.loop(1, row_count)
        def _(by):
            all_copy(s, by).wait_send()

        sum_out(s).wait()


def close(y_ref, t_ref, diag_ref, new_ref, out_ref, y, t, diag, y_sem, t_sem, diag_sem, new_sem, out_sem):
    supers = y_ref.shape[0]

    def copy(src, dst, sem):
        return pltpu.make_async_copy(src, dst, sem)

    t_in, diag_in = copy(t_ref, t, t_sem), copy(diag_ref, diag, diag_sem)
    half = y_ref.shape[1] // 2
    parts = [(s, pl.ds(h * half, half)) for s in range(supers) for h in range(2)]
    y_in = [copy(y_ref.at[at], y.at[at], y_sem.at[i]) for i, at in enumerate(parts)]
    y_over = [copy(y.at[at], new_ref.at[at], new_sem.at[i]) for i, at in enumerate(parts)]
    for each in y_in + [t_in, diag_in]:
        each.start()
    for came, goes in zip(y_in, y_over):
        came.wait()
        goes.start()
    t_in.wait()
    diag_in.wait()
    diag[...] += t[...].astype(F32)
    over = copy(diag, out_ref, out_sem)
    over.start()
    for each in y_over + [over]:
        each.wait()


def fused(resident_inverse, factor, diag_inverse, anc_tiles, slot_tile):
    own_rows, own_cols = resident_inverse.shape
    supers, _, width = factor.shape
    row_count, col_count = lax.axis_size("row"), lax.axis_size("col")
    total_rows = own_rows * row_count
    row_mask = slot_rows(anc_tiles, slot_tile, total_rows // slot_tile.shape[0])
    own_mask = lax.dynamic_slice_in_dim(row_mask, lax.axis_index("row") * own_rows, own_rows, 1)
    piece = own_cols // row_count
    owners = row_count // CORES
    passes = col_count * supers
    wide = width * col_count
    dma = pltpu.SemaphoreType.DMA
    y, t = pl.pallas_call(
        lambda *refs: sweep(row_count, col_count, supers, *refs),
        out_shape=(
            jax.ShapeDtypeStruct((supers, own_rows, width), BF),
            jax.ShapeDtypeStruct((supers, row_count, wide // row_count, width), BF),
        ),
        in_specs=[pl.BlockSpec(memory_space=pl.ANY)] * 2 + [pl.BlockSpec(memory_space=pltpu.VMEM)],
        out_specs=[pl.BlockSpec(memory_space=pl.ANY)] * 2,
        scratch_shapes=[
            pltpu.VMEM((supers, own_rows, width), BF),
            pltpu.VMEM((wide, width), F32),
            pltpu.VMEM((DEPTH, own_rows, piece), BF),
            pltpu.VMEM((supers, col_count, width, own_rows), BF),
            pltpu.VMEM((2, CHIPS, width, piece), BF),
            pltpu.VMEM((passes, CHIPS, width, piece), BF),
            pltpu.VMEM((2, CHIPS, width, piece), BF),
            pltpu.VMEM((passes, CHIPS - 1, width, piece), BF),
            pltpu.VMEM((supers, 2 * col_count, width, piece), BF),
            pltpu.VMEM((supers, owners, width, piece), BF),
            pltpu.VMEM((supers, row_count, wide // row_count, width), BF),
            pltpu.VMEM((supers, row_count, wide // row_count, width), BF),
            pltpu.VMEM((supers, wide // row_count, width), BF),
            dma((DEPTH,)), dma((supers,)), dma((2, supers)),
            dma((2, supers, col_count)), dma((supers, col_count)),
            dma((2, CHIPS)), dma((passes, CHIPS)),
            dma((2, CHIPS)), dma((passes, CHIPS)),
            dma((supers, col_count, STRIPS)), dma((supers, col_count, STRIPS)),
            dma((supers, col_count, STRIPS)), dma((supers, owners, STRIPS)),
            dma((supers, row_count)), dma((supers, row_count)),
            dma((supers, row_count)), dma((supers, row_count)),
            pltpu.SemaphoreType.REGULAR((2,)),
        ],
        compiler_params=pltpu.CompilerParams(
            collective_id=0, has_side_effects=True, vmem_limit_bytes=67043328
        ),
    )(factor, resident_inverse, own_mask[:, None, :])
    t = t.reshape(diag_inverse.shape)
    return tuple(pl.pallas_call(
        close,
        in_specs=[pl.BlockSpec(memory_space=pl.ANY)] * 3,
        out_specs=[pl.BlockSpec(memory_space=pl.ANY)] * 2,
        out_shape=(jax.ShapeDtypeStruct(y.shape, BF), jax.ShapeDtypeStruct(t.shape, F32)),
        scratch_shapes=[
            pltpu.VMEM(y.shape, BF), pltpu.VMEM(t.shape, BF), pltpu.VMEM(t.shape, F32),
            dma((2 * supers,)), dma(()), dma(()), dma((2 * supers,)), dma(()),
        ],
    )(y, t, diag_inverse))


def on_device(*arrays):
    square = lax.axis_size("row") == CHIPS * CORES and lax.axis_size("col") == CHIPS
    return (fused if square else plain)(*arrays)


def solution(mesh):
    placed = (P("row", "col"), P(None, "row", "col"), P(None, None, "col"), P(), P())
    return jax.shard_map(
        on_device,
        mesh=mesh,
        in_specs=placed,
        out_specs=(P(None, "row", "col"), P(None, None, "col")),
        check_vma=False,
    )
```
